256 devices in a mesh: kmer: 16 (over y, z_hi), samp: 16 (over z_lo, x, core).
Axes of the slice: x: 4, y: 4, z: 8 (z_hi: 4, z_lo: 2; z = z_hi * 2 + z_lo), core: 2. Of those that a mesh axis runs over, the one named last changes fastest.
Arguments:
- tiles: bfloat16 [22528, 128, 128], P(('kmer', 'samp')), may hold values from 0 to 8
- omega: bfloat16 [16384, 128], P('samp'), may hold values from -0.5 to 0.5
- tile_rows: int32 [22528], P(('kmer', 'samp')), may hold values from 0 to 55, as said below
- tile_cols: int32 [22528], P(('kmer', 'samp')), may hold values from 0 to 7
- tile_count: int32 [256], P(('kmer', 'samp')), may hold values from 11 to 88, as said below
Outputs:
- sketch: bfloat16 [114688, 128], P(('kmer', 'samp'))
- co_sketch: float32 [16384, 128], P(('samp', 'kmer'))
The draws below stay inside these ranges and needn't reach their ends.
Inputs may be any that keep to these rules, and one draw needn't show every extreme that they name: `tile_rows`: on each device the used slots name distinct pairs of k-mer block and sample block. `tile_count`: at least one device uses all 88 slots.
All inputs are finite; a program needn't handle non-finite values.
Results may differ from the reference program's by a relative error of at most 0.014.
Values may be sent and summed in bfloat16 or wider, within the bound.
No kernel may reach another device: no remote copies, remote signals or barrier semaphores. Data moves between devices by JAX's collectives and lax.ppermute only.
A program may use at most 64 MiB of HBM per device.

```python
import jax
import jax.numpy as jnp
from jax import lax

TILE = 128
RANK = 128
SB_DEV = 8
KB_DEV = 56
CAP = 88
KMERS = 114688
SAMPLES = 16384
N_KMER = 16
N_SAMP = 16
DEVICES = 256


def tile_plan(key):
    base = jax.random.fold_in(key, 7)
    key_a, key_b, key_c, key_d, key_e = jax.random.split(base, 5)
    slot_total = KB_DEV * SB_DEV
    scores = jax.random.randint(key_a, (DEVICES, slot_total), 0, 2 ** 19) * slot_total
    scores = scores + jnp.arange(slot_total, dtype=jnp.int32)[None, :]
    order = jnp.argsort(scores, axis=1)[:, :CAP].astype(jnp.int32)
    rows = (order // SB_DEV).reshape(DEVICES * CAP).astype(jnp.int32)
    cols = (order % SB_DEV).reshape(DEVICES * CAP).astype(jnp.int32)
    counts = jax.random.randint(key_b, (DEVICES,), CAP // 8, CAP // 4 + 1)
    heavy = jax.random.randint(key_c, (DEVICES,), 0, 8) == 0
    counts = jnp.where(heavy, CAP, counts)
    first = jax.random.randint(key_d, (), 0, DEVICES)
    second = (first + 1 + jax.random.randint(key_e, (), 0, DEVICES - 1)) % DEVICES
    counts = counts.at[first].set(CAP)
    counts = counts.at[second].set(CAP // 8)
    return (rows, cols, counts.astype(jnp.int32))


def draw_tile_rows(key, part):
    return tile_plan(key)[0]


def draw_tile_cols(key, part):
    return tile_plan(key)[1]


def draw_tile_count(key, part):
    return tile_plan(key)[2]


def draw_tiles(key, part):
    base = jax.random.fold_in(key, 11)
    key_mask, key_value = jax.random.split(base, 2)
    shape = (DEVICES * CAP, TILE, TILE)
    picker = jax.random.uniform(key_mask, shape, jnp.float32)
    level = jax.random.uniform(key_value, shape, jnp.float32)
    values = 8.0 * level
    values = jnp.where(picker < 0.05, values, jnp.float32(0.0))
    return jnp.clip(values, 0.0, 8.0).astype(jnp.bfloat16)


def level_of(rng, shape, shards, smallest, high):
    def one(position, parts):
        heights = jax.random.uniform(jax.random.fold_in(jax.random.fold_in(rng, 6), position), (parts,), jnp.float32, smallest / len(shards), high / len(shards))
        return jnp.repeat(jnp.exp(heights), shape[position] // parts).reshape((-1,) + (1,) * (len(shape) - position - 1))

    level = one(*shards[0])
    for cut in shards[1:]:
        level = level * one(*cut)
    return level


def noise(rng, extent, scale, most, shards=(), kind=jnp.bfloat16):
    loudness = level_of(rng, extent, shards, -0.22, 0.18) if shards else 1.0
    entries = jax.random.normal(rng, extent, jnp.float32) * scale * loudness
    return jnp.minimum(jnp.maximum(entries, -most), most).astype(kind)


def setup_inputs(seed: int = 0) -> dict:
    keys = jax.random.split(jax.random.key(seed), 6)
    tiles = draw_tiles(jax.random.fold_in(keys[5], 71), 0)
    omega = noise(keys[1], (SAMPLES, RANK), (4 * (SB_DEV * TILE * N_SAMP) ** -0.5), 0.5, ((0, 16),))
    tile_rows = draw_tile_rows(jax.random.fold_in(keys[5], 71), 0)
    tile_cols = draw_tile_cols(jax.random.fold_in(keys[5], 71), 0)
    tile_count = draw_tile_count(jax.random.fold_in(keys[5], 71), 0)
    return {"tiles": tiles, "omega": omega, "tile_rows": tile_rows, "tile_cols": tile_cols, "tile_count": tile_count}


def reference(tiles, omega, tile_rows, tile_cols, tile_count):
    tile_grid = tiles.reshape(N_KMER, N_SAMP, CAP, TILE, TILE)
    row_grid = tile_rows.reshape(N_KMER, N_SAMP, CAP)
    col_grid = tile_cols.reshape(N_KMER, N_SAMP, CAP)
    count_grid = tile_count.reshape(N_KMER, N_SAMP)
    omega_grid = omega.reshape(N_SAMP, SB_DEV, TILE, RANK)
    slots = jnp.arange(CAP, dtype=jnp.int32)

    def sketch_rows(kidx):
        def add_part(total, sidx):
            block = tile_grid[kidx, sidx].astype(jnp.float32)
            chosen = omega_grid[sidx][col_grid[kidx, sidx]].astype(jnp.float32)
            prod = jnp.einsum('tkc,tcr->tkr', block, chosen)
            live = slots < count_grid[kidx, sidx]
            prod = jnp.where(live[:, None, None], prod, jnp.float32(0.0))
            part = jax.ops.segment_sum(prod, row_grid[kidx, sidx], num_segments=KB_DEV)
            rounded = lax.optimization_barrier(part.astype(jnp.bfloat16))
            return total + rounded.astype(jnp.float32), None

        start = jnp.zeros((KB_DEV, TILE, RANK), jnp.float32)
        total, _ = lax.scan(add_part, start, jnp.arange(N_SAMP, dtype=jnp.int32))
        return total.astype(jnp.bfloat16)

    sketch_grid = lax.map(sketch_rows, jnp.arange(N_KMER, dtype=jnp.int32))

    def co_rows(sidx):
        def add_part(total, kidx):
            block = tile_grid[kidx, sidx].astype(jnp.float32)
            chosen = sketch_grid[kidx][row_grid[kidx, sidx]].astype(jnp.float32)
            prod = jnp.einsum('tkc,tkr->tcr', block, chosen)
            live = slots < count_grid[kidx, sidx]
            prod = jnp.where(live[:, None, None], prod, jnp.float32(0.0))
            part = jax.ops.segment_sum(prod, col_grid[kidx, sidx], num_segments=SB_DEV)
            return total + part, None

        start = jnp.zeros((SB_DEV, TILE, RANK), jnp.float32)
        total, _ = lax.scan(add_part, start, jnp.arange(N_KMER, dtype=jnp.int32))
        return total * jnp.float32(1.0 / (KMERS ** 0.5))

    co_grid = lax.map(co_rows, jnp.arange(N_SAMP, dtype=jnp.int32))
    return sketch_grid.reshape(KMERS, RANK), co_grid.reshape(SAMPLES, RANK)
```

```python
import functools

import jax
import jax.numpy as jnp
from jax import lax
from jax.experimental import pallas as pl
from jax.experimental.pallas import tpu as pltpu
from jax.sharding import PartitionSpec as P

TILE = 128
KB_DEV = 56
SB_DEV = 8
HALF_BLOCKS = KB_DEV // 2
HALF = HALF_BLOCKS * TILE
CHUNK = HALF // 8
UNROLL = 4
VMEM_LIMIT = 48 * 1024 * 1024

ROUNDS = (
    ((2, 1), (2, 1)),
    ((1, 1), (3, 0)),
    ((3, 0), (1, 1)),
    ((1, 0), (3, 1)),
    ((3, 1), (1, 0)),
    ((2, 0), (0, 1)),
    ((0, 1), (2, 0)),
)


def vm():
    return pl.BlockSpec(memory_space=pltpu.VMEM)


def sm():
    return pl.BlockSpec(memory_space=pltpu.SMEM)


def params():
    return pltpu.CompilerParams(vmem_limit_bytes=VMEM_LIMIT)


def place():
    j = lax.axis_index("samp")
    return j // 8, (j // 2) % 4, j % 2


def pairs(r):
    out = []
    for s in range(16):
        z, x, c = s // 8, (s // 2) % 4, s % 2
        dx, dz = ROUNDS[r][c]
        out.append((s, (z ^ dz) * 8 + ((x + dx) % 4) * 2 + c))
    return out


def peer_chunk(r, sign):
    z, x, c = place()
    (dx0, dz0), (dx1, dz1) = ROUNDS[r]
    dx = jnp.where(c == 0, dx0, dx1) * sign
    dz = jnp.where(c == 0, dz0, dz1)
    zz = z + dz - 2 * z * dz
    return zz * 4 + (x + dx + 4) % 4


def select_slots(rows, cols, count, half, l_slot, l_row, l_col):
    def visit(s, n):
        row = rows[s] - half * HALF_BLOCKS
        l_slot[n] = s
        l_row[n] = row
        l_col[n] = cols[s]
        mine = jnp.logical_and(row >= 0, row < HALF_BLOCKS)
        return n + mine.astype(jnp.int32)

    n = lax.fori_loop(0, count[0], visit, jnp.int32(0))
    for u in range(UNROLL):
        l_slot[n + u] = 0
        l_row[n + u] = HALF_BLOCKS
        l_col[n + u] = SB_DEV
    return n


def block(i):
    return pl.ds(pl.multiple_of(i * TILE, TILE), TILE)


def forward_kernel(mine, rows, cols, count, tiles, omega, out, acc, l_slot, l_row, l_col):
    _, _, c = place()
    half = c if mine else 1 - c
    n = select_slots(rows, cols, count, half, l_slot, l_row, l_col)
    acc[...] = jnp.zeros_like(acc)

    def step(g, carry):
        prods = []
        for u in range(UNROLL):
            k = g * UNROLL + u
            col = jnp.minimum(l_col[k], SB_DEV - 1)
            prods.append(
                jnp.dot(tiles[l_slot[k]], omega[block(col), :], preferred_element_type=jnp.float32)
            )
        for u in range(UNROLL):
            where = block(l_row[g * UNROLL + u])
            acc[where, :] = acc[where, :] + prods[u]
        return carry

    lax.fori_loop(0, (n + UNROLL - 1) // UNROLL, step, 0)
    out[...] = acc[pl.ds(0, HALF), :].astype(jnp.bfloat16)


def forward(mine, rows, cols, count, tiles, omega):
    cap = tiles.shape[0]
    return pl.pallas_call(
        functools.partial(forward_kernel, mine),
        out_shape=jax.ShapeDtypeStruct((HALF, TILE), jnp.bfloat16),
        in_specs=[sm(), sm(), sm(), vm(), vm()],
        out_specs=vm(),
        scratch_shapes=[pltpu.VMEM((HALF + TILE, TILE), jnp.float32)]
        + [pltpu.SMEM((cap + UNROLL,), jnp.int32)] * 3,
        compiler_params=params(),
        name="forward_mine" if mine else "forward_other",
    )(rows, cols, count, tiles, omega)


def turn_kernel(tiles, out):
    def one(s, carry):
        out[s] = tiles[s].T
        return carry

    lax.fori_loop(0, tiles.shape[0], one, 0, unroll=4)


def turn(tiles):
    return pl.pallas_call(
        turn_kernel,
        out_shape=jax.ShapeDtypeStruct(tiles.shape, tiles.dtype),
        in_specs=[vm()],
        out_specs=vm(),
        compiler_params=params(),
        name="turn_tiles",
    )(tiles)


def chunk_at(i):
    return pl.ds(pl.multiple_of(i * CHUNK, CHUNK), CHUNK)


def pair_kernel(a, b, own, *sends):
    def total(i):
        at = chunk_at(i)
        return (a[at, :].astype(jnp.float32) + b[at, :].astype(jnp.float32)).astype(jnp.bfloat16)

    z, x, _ = place()
    for r, send in enumerate(sends):
        send[...] = total(peer_chunk(r, 1))
    own[...] = total(z * 4 + x)


def pair_sum(a, b):
    shape = jax.ShapeDtypeStruct((CHUNK, TILE), jnp.bfloat16)
    return pl.pallas_call(
        pair_kernel,
        out_shape=[shape] * 8,
        in_specs=[vm(), vm()],
        out_specs=[vm()] * 8,
        compiler_params=params(),
        name="pair_sum",
    )(a, b)


def chunk_kernel(*refs):
    out = refs[-1]
    total = refs[0][...].astype(jnp.float32)
    for ref in refs[1:-1]:
        total = total + ref[...].astype(jnp.float32)
    out[...] = total.astype(jnp.bfloat16)


def chunk_sum(parts):
    return pl.pallas_call(
        chunk_kernel,
        out_shape=jax.ShapeDtypeStruct((CHUNK, TILE), jnp.bfloat16),
        in_specs=[vm()] * len(parts),
        out_specs=vm(),
        compiler_params=params(),
        name="chunk_sum",
    )(*parts)


def gather_kernel(*refs):
    z, x, _ = place()
    out = refs[-1]
    out[chunk_at(z * 4 + x), :] = refs[0][...]
    for r, ref in enumerate(refs[1:-1]):
        out[chunk_at(peer_chunk(r, -1)), :] = ref[...]


def gather_half(own, got):
    return pl.pallas_call(
        gather_kernel,
        out_shape=jax.ShapeDtypeStruct((HALF, TILE), jnp.bfloat16),
        in_specs=[vm()] * 8,
        out_specs=vm(),
        compiler_params=params(),
        name="gather_half",
    )(own, *got)


def backward_slots(n, l_slot, l_row, l_col, turned, table, acc):
    def step(g, carry):
        prods = []
        for u in range(UNROLL):
            k = g * UNROLL + u
            row = jnp.minimum(l_row[k], HALF_BLOCKS - 1)
            prods.append(
                jnp.dot(turned[l_slot[k]], table[block(row), :], preferred_element_type=jnp.float32)
            )
        for u in range(UNROLL):
            where = block(l_col[g * UNROLL + u])
            acc[where, :] = acc[where, :] + prods[u]
        return carry

    lax.fori_loop(0, (n + UNROLL - 1) // UNROLL, step, 0)


def backward_mine_kernel(rows, cols, count, turned, table, out, l_slot, l_row, l_col):
    _, _, c = place()
    n = select_slots(rows, cols, count, c, l_slot, l_row, l_col)
    out[...] = jnp.zeros_like(out)
    backward_slots(n, l_slot, l_row, l_col, turned, table, out)


def backward_mine(rows, cols, count, turned, table):
    cap = turned.shape[0]
    return pl.pallas_call(
        backward_mine_kernel,
        out_shape=jax.ShapeDtypeStruct(((SB_DEV + 1) * TILE, TILE), jnp.float32),
        in_specs=[sm(), sm(), sm(), vm(), vm()],
        out_specs=vm(),
        scratch_shapes=[pltpu.SMEM((cap + UNROLL,), jnp.int32)] * 3,
        compiler_params=params(),
        name="backward_mine",
    )(rows, cols, count, turned, table)


def backward_other_kernel(
    rows, cols, count, turned, first, own, table, out, sketch, acc, l_slot, l_row, l_col
):
    z, x, c = place()
    n = select_slots(rows, cols, count, 1 - c, l_slot, l_row, l_col)
    acc[...] = first[...]
    backward_slots(n, l_slot, l_row, l_col, turned, table, acc)
    out[...] = acc[pl.ds(0, SB_DEV * TILE), :].astype(jnp.bfloat16)
    at = chunk_at(x * 2 + c)

    @pl.when(z == c)
    def _():
        sketch[...] = own[at, :]

    @pl.when(z != c)
    def _():
        sketch[...] = table[at, :]


def backward_other(rows, cols, count, turned, first, own, table):
    cap = turned.shape[0]
    return pl.pallas_call(
        backward_other_kernel,
        out_shape=[
            jax.ShapeDtypeStruct((SB_DEV * TILE, TILE), jnp.bfloat16),
            jax.ShapeDtypeStruct((CHUNK, TILE), jnp.bfloat16),
        ],
        in_specs=[sm(), sm(), sm(), vm(), vm(), vm(), vm()],
        out_specs=[vm(), vm()],
        scratch_shapes=[pltpu.VMEM(((SB_DEV + 1) * TILE, TILE), jnp.float32)]
        + [pltpu.SMEM((cap + UNROLL,), jnp.int32)] * 3,
        compiler_params=params(),
        name="backward_other",
    )(rows, cols, count, turned, first, own, table)


def last_kernel(factor, parts, out):
    total = parts[0].astype(jnp.float32)
    for i in range(1, parts.shape[0]):
        total = total + parts[i].astype(jnp.float32)
    out[...] = total * factor


def last_sum(factor, parts):
    return pl.pallas_call(
        functools.partial(last_kernel, factor),
        out_shape=jax.ShapeDtypeStruct(parts.shape[1:], jnp.float32),
        in_specs=[vm()],
        out_specs=vm(),
        compiler_params=params(),
        name="last_sum",
    )(parts)


def shards(tiles, omega, tile_rows, tile_cols, tile_count):
    swap = [(s, s ^ 1) for s in range(16)]
    kmers = lax.axis_size("kmer")
    other = forward(False, tile_rows, tile_cols, tile_count, tiles, omega)
    mine = forward(True, tile_rows, tile_cols, tile_count, tiles, omega)
    got = lax.ppermute(other, "samp", swap)
    own, *sends = pair_sum(mine, got)
    turned = turn(tiles)
    parts = [lax.ppermute(s, "samp", pairs(r)) for r, s in enumerate(sends)]
    chunk = chunk_sum([own, *parts])
    pieces = [lax.ppermute(chunk, "samp", pairs(r)) for r in range(7)]
    own_half = gather_half(chunk, pieces)
    other_half = lax.ppermute(own_half, "samp", swap)
    first = backward_mine(tile_rows, tile_cols, tile_count, turned, own_half)
    zpart, sketch = backward_other(
        tile_rows, tile_cols, tile_count, turned, first, own_half, other_half
    )
    shares = lax.all_to_all(zpart.reshape(kmers, -1, TILE), "kmer", 0, 0)
    factor = 1.0 / (KB_DEV * TILE * kmers) ** 0.5
    return sketch, last_sum(factor, shares)


def solution(mesh):
    placed = (
        P(("kmer", "samp"), None, None),
        P("samp", None),
        P(("kmer", "samp")),
        P(("kmer", "samp")),
        P(("kmer", "samp")),
    )
    return jax.shard_map(
        shards,
        mesh=mesh,
        in_specs=placed,
        out_specs=(P(("kmer", "samp"), None), P(("samp", "kmer"), None)),
        check_vma=False,
    )
```

```python
import functools

import jax
import jax.numpy as jnp
from jax import lax
from jax.experimental import pallas as pl
from jax.experimental.pallas import tpu as pltpu
from jax.sharding import PartitionSpec as P

TILE = 128
KB_DEV = 56
SB_DEV = 8
HALF_BLOCKS = KB_DEV // 2
HALF = HALF_BLOCKS * TILE
CHUNK = HALF // 8
UNROLL = 12
LIST = 128
VMEM_LIMIT = 48 * 1024 * 1024

ROUNDS = (
    ((2, 1), (2, 1)),
    ((1, 1), (3, 0)),
    ((3, 0), (1, 1)),
    ((1, 0), (3, 1)),
    ((3, 1), (1, 0)),
    ((2, 0), (0, 1)),
    ((0, 1), (2, 0)),
)

LINE = ((1, 3), (3, 1), (2, 2))


def vm():
    return pl.BlockSpec(memory_space=pltpu.VMEM)


def sm():
    return pl.BlockSpec(memory_space=pltpu.SMEM)


def params():
    return pltpu.CompilerParams(vmem_limit_bytes=VMEM_LIMIT)


def place():
    j = lax.axis_index("samp")
    return j // 8, (j // 2) % 4, j % 2


def pairs(r):
    out = []
    for s in range(16):
        z, x, c = s // 8, (s // 2) % 4, s % 2
        dx, dz = ROUNDS[r][c]
        out.append((s, (z ^ dz) * 8 + ((x + dx) % 4) * 2 + c))
    return out


def peer_chunk(r, sign):
    z, x, c = place()
    (dx0, dz0), (dx1, dz1) = ROUNDS[r]
    dx = jnp.where(c == 0, dx0, dx1) * sign
    dz = jnp.where(c == 0, dz0, dz1)
    zz = z + dz - 2 * z * dz
    return zz * 4 + (x + dx + 4) % 4


def block(i):
    return pl.ds(pl.multiple_of(i * TILE, TILE), TILE)


def unpack(word):
    return lax.rem(word, 128), lax.rem(lax.div(word, 128), 64), lax.div(word, 8192)


def list_slots(rows, cols, count, base, far, near):
    cap = rows.shape[0]

    def visit(s, carry):
        n_far, n_near = carry
        row = rows[s] - base
        inside = jnp.logical_and(row >= 0, row < HALF_BLOCKS)
        within = jnp.where(inside, row, rows[s] - (HALF_BLOCKS - base))
        word = s + within * 128 + cols[s] * 8192
        far[n_far] = word
        near[n_near] = word
        used = (s < count).astype(jnp.int32)
        here = inside.astype(jnp.int32)
        return n_far + used * (1 - here), n_near + used * here

    n_far, n_near = lax.fori_loop(0, cap, visit, (jnp.int32(0), jnp.int32(0)), unroll=8)
    pad = HALF_BLOCKS * 128 + SB_DEV * 8192
    pad_far, pad_near = pad + lax.rem(far[0], 128), pad + lax.rem(near[0], 128)
    for u in range(UNROLL):
        far[n_far + u] = pad_far
        near[n_near + u] = pad_near
    far[LIST - 1] = n_far
    near[LIST - 1] = n_near
    return n_far, n_near


def forward_slots(n, entries, tiles, omega, acc, out):
    acc[...] = jnp.zeros_like(acc)

    def step(g, carry):
        prods, where = [], []
        for u in range(UNROLL):
            slot, row, col = unpack(entries[g * UNROLL + u])
            col = jnp.minimum(col, SB_DEV - 1)
            where.append(block(row))
            prods.append(
                jnp.dot(tiles[slot], omega[block(col), :], preferred_element_type=jnp.float32)
            )
        for at, prod in zip(where, prods):
            acc[at, :] = acc[at, :] + prod
        return carry

    lax.fori_loop(0, (n + UNROLL - 1) // UNROLL, step, 0)
    out[...] = acc[pl.ds(0, HALF), :].astype(jnp.bfloat16)


def forward_far_kernel(
    rows, cols, count, tiles, omega, out, held, table, far, near, acc, s_rows, s_cols, sems
):
    small = [
        pltpu.make_async_copy(rows, s_rows, sems.at[0]),
        pltpu.make_async_copy(cols, s_cols, sems.at[1]),
    ]
    for copy in small:
        copy.start()
    fetch_omega = pltpu.make_async_copy(omega, table, sems.at[2])
    fetch_omega.start()
    for copy in small:
        copy.wait()
    _, _, c = place()
    n_far, n_near = list_slots(s_rows, s_cols, count[0], c * HALF_BLOCKS, far, near)

    def fetch(entries, sem, k):
        slot = lax.rem(entries[k], 128)
        return pltpu.make_async_copy(tiles.at[slot], held.at[slot], sem)

    def start(entries, sem, n):
        def one(k, carry):
            fetch(entries, sem, k).start()
            return carry

        lax.fori_loop(0, n, one, 0)

    def wait(entries, sem, n):
        def one(k, carry):
            fetch(entries, sem, k).wait()
            return carry

        lax.fori_loop(0, n, one, 0)

    start(far, sems.at[3], n_far)
    start(near, sems.at[4], n_near)
    fetch_omega.wait()
    wait(far, sems.at[3], n_far)
    forward_slots(n_far, far, held, table, acc, out)
    wait(near, sems.at[4], n_near)


def forward_far(rows, cols, count, tiles, omega):
    cap = tiles.shape[0]
    anywhere = pl.BlockSpec(memory_space=pltpu.HBM)
    entries = jax.ShapeDtypeStruct((LIST,), jnp.int32)
    return pl.pallas_call(
        forward_far_kernel,
        out_shape=[
            jax.ShapeDtypeStruct((HALF, TILE), jnp.bfloat16),
            jax.ShapeDtypeStruct(tiles.shape, tiles.dtype),
            jax.ShapeDtypeStruct(omega.shape, omega.dtype),
            entries,
            entries,
        ],
        in_specs=[anywhere, anywhere, sm(), anywhere, anywhere],
        out_specs=[vm(), vm(), vm(), sm(), sm()],
        scratch_shapes=[
            pltpu.VMEM((HALF + TILE, TILE), jnp.float32),
            pltpu.SMEM((cap,), jnp.int32),
            pltpu.SMEM((cap,), jnp.int32),
            pltpu.SemaphoreType.DMA((5,)),
        ],
        compiler_params=params(),
        name="forward_far",
    )(*(pltpu.with_memory_space_constraint(v, pltpu.HBM) for v in (rows, cols)), count,
      *(pltpu.with_memory_space_constraint(v, pltpu.HBM) for v in (tiles, omega)))


def forward_near_kernel(near, held, table, out, acc):
    forward_slots(near[LIST - 1], near, held, table, acc, out)


def forward_near(near, held, table):
    return pl.pallas_call(
        forward_near_kernel,
        out_shape=jax.ShapeDtypeStruct((HALF, TILE), jnp.bfloat16),
        in_specs=[sm(), vm(), vm()],
        out_specs=vm(),
        scratch_shapes=[pltpu.VMEM((HALF + TILE, TILE), jnp.float32)],
        compiler_params=params(),
        name="forward_near",
    )(near, held, table)


def turn_kernel(far, near, tiles, out):
    def one(g, carry):
        for u in range(4):
            out[g * 4 + u] = tiles[g * 4 + u].T
        return carry

    lax.fori_loop(0, (far[LIST - 1] + near[LIST - 1] + 3) // 4, one, 0)


def turn(far, near, tiles):
    return pl.pallas_call(
        turn_kernel,
        out_shape=jax.ShapeDtypeStruct(tiles.shape, tiles.dtype),
        in_specs=[sm(), sm(), vm()],
        out_specs=vm(),
        compiler_params=params(),
        name="turn_tiles",
    )(far, near, tiles)


def chunk_at(i):
    return pl.ds(pl.multiple_of(i * CHUNK, CHUNK), CHUNK)


def pair_kernel(a, b, own, *sends):
    def total(i):
        at = chunk_at(i)
        return (a[at, :].astype(jnp.float32) + b[at, :].astype(jnp.float32)).astype(jnp.bfloat16)

    z, x, _ = place()
    for r, send in enumerate(sends):
        send[...] = total(peer_chunk(r, 1))
    own[...] = total(z * 4 + x)


def pair_sum(a, b):
    shape = jax.ShapeDtypeStruct((CHUNK, TILE), jnp.bfloat16)
    return pl.pallas_call(
        pair_kernel,
        out_shape=[shape] * 8,
        in_specs=[vm(), vm()],
        out_specs=[vm()] * 8,
        compiler_params=params(),
        name="pair_sum",
    )(a, b)


def chunk_kernel(*refs):
    out = refs[-1]
    total = refs[0][...].astype(jnp.float32)
    for ref in refs[1:-1]:
        total = total + ref[...].astype(jnp.float32)
    out[...] = total.astype(jnp.bfloat16)


def chunk_sum(parts):
    return pl.pallas_call(
        chunk_kernel,
        out_shape=jax.ShapeDtypeStruct((CHUNK, TILE), jnp.bfloat16),
        in_specs=[vm()] * len(parts),
        out_specs=vm(),
        compiler_params=params(),
        name="chunk_sum",
    )(*parts)


def gather_kernel(*refs):
    z, x, _ = place()
    out = refs[-1]
    out[chunk_at(z * 4 + x), :] = refs[0][...]
    for r, ref in enumerate(refs[1:-1]):
        out[chunk_at(peer_chunk(r, -1)), :] = ref[...]


def gather_half(own, got):
    return pl.pallas_call(
        gather_kernel,
        out_shape=jax.ShapeDtypeStruct((HALF, TILE), jnp.bfloat16),
        in_specs=[vm()] * 8,
        out_specs=vm(),
        compiler_params=params(),
        name="gather_half",
    )(own, *got)


def backward_slots(n, entries, turned, table, acc):
    def step(g, carry):
        prods, where = [], []
        for u in range(UNROLL):
            slot, row, col = unpack(entries[g * UNROLL + u])
            row = jnp.minimum(row, HALF_BLOCKS - 1)
            where.append(block(col))
            prods.append(
                jnp.dot(turned[slot], table[block(row), :], preferred_element_type=jnp.float32)
            )
        for at, prod in zip(where, prods):
            acc[at, :] = acc[at, :] + prod
        return carry

    lax.fori_loop(0, (n + UNROLL - 1) // UNROLL, step, 0)


def backward_near_kernel(near, turned, table, out):
    out[...] = jnp.zeros_like(out)
    backward_slots(near[LIST - 1], near, turned, table, out)


def backward_near(near, turned, table):
    return pl.pallas_call(
        backward_near_kernel,
        out_shape=jax.ShapeDtypeStruct(((SB_DEV + 1) * TILE, TILE), jnp.float32),
        in_specs=[sm(), vm(), vm()],
        out_specs=vm(),
        compiler_params=params(),
        name="backward_near",
    )(near, turned, table)


def line_offset(r, sign):
    _, _, c = place()
    return jnp.where(c == 0, LINE[r][0], LINE[r][1]) * sign


def share_at(i, size):
    return pl.ds(pl.multiple_of(lax.rem(i + 4, 4) * size, size), size)


def kmer_place():
    i = lax.axis_index("kmer")
    return i // 4, i % 4


def backward_far_kernel(far, turned, first, own, table, keep, s0, s1, s2, sketch, acc):
    acc[...] = first[...]
    backward_slots(far[LIST - 1], far, turned, table, acc)
    y, _ = kmer_place()
    size = keep.shape[0]
    for r, send in enumerate((s0, s1, s2)):
        send[...] = acc[share_at(y + line_offset(r, 1), size), :].astype(jnp.bfloat16)
    keep[...] = acc[share_at(y, size), :]
    z, x, c = place()
    at = chunk_at(x * 2 + c)

    @pl.when(z == c)
    def _():
        sketch[...] = own[at, :]

    @pl.when(z != c)
    def _():
        sketch[...] = table[at, :]


def backward_far(far, turned, first, own, table):
    share = SB_DEV * TILE // 4
    send = jax.ShapeDtypeStruct((share, TILE), jnp.bfloat16)
    return pl.pallas_call(
        backward_far_kernel,
        out_shape=[
            jax.ShapeDtypeStruct((share, TILE), jnp.float32),
            send,
            send,
            send,
            jax.ShapeDtypeStruct((CHUNK, TILE), jnp.bfloat16),
        ],
        in_specs=[sm(), vm(), vm(), vm(), vm()],
        out_specs=[vm()] * 5,
        scratch_shapes=[pltpu.VMEM(((SB_DEV + 1) * TILE, TILE), jnp.float32)],
        compiler_params=params(),
        name="backward_far",
    )(far, turned, first, own, table)


def line_kernel(own, g0, g1, g2, keep, s0, s1, s2, acc):
    total = own[...]
    for got in (g0, g1, g2):
        total = total + got[...].astype(jnp.float32)
    acc[...] = total
    _, zh = kmer_place()
    size = keep.shape[0]
    for r, send in enumerate((s0, s1, s2)):
        send[...] = acc[share_at(zh + line_offset(r, 1), size), :].astype(jnp.bfloat16)
    keep[...] = acc[share_at(zh, size), :]


def line_sum(own, got):
    share = own.shape[0] // 4
    send = jax.ShapeDtypeStruct((share, TILE), jnp.bfloat16)
    return pl.pallas_call(
        line_kernel,
        out_shape=[jax.ShapeDtypeStruct((share, TILE), jnp.float32), send, send, send],
        in_specs=[vm()] * 4,
        out_specs=[vm()] * 4,
        scratch_shapes=[pltpu.VMEM(own.shape, jnp.float32)],
        compiler_params=params(),
        name="line_sum",
    )(own, *got)


def last_kernel(factor, own, g0, g1, g2, out):
    total = own[...]
    for got in (g0, g1, g2):
        total = total + got[...].astype(jnp.float32)
    out[...] = total * factor


def last_sum(factor, own, got):
    return pl.pallas_call(
        functools.partial(last_kernel, factor),
        out_shape=jax.ShapeDtypeStruct(own.shape, jnp.float32),
        in_specs=[vm()] * 4,
        out_specs=vm(),
        compiler_params=params(),
        name="last_sum",
    )(own, *got)


def line_permute(value, r, along_y):
    out = []
    for i in range(16):
        for j in range(16):
            y, zh = i // 4, i % 4
            off = LINE[r][j % 2]
            to = ((y + off) % 4) * 4 + zh if along_y else y * 4 + (zh + off) % 4
            out.append((i * 16 + j, to * 16 + j))
    return lax.ppermute(value, ("kmer", "samp"), out)


def shards(tiles, omega, tile_rows, tile_cols, tile_count):
    swap = [(s, s ^ 1) for s in range(16)]
    kmers = lax.axis_size("kmer")
    other, held, table, far, near = forward_far(tile_rows, tile_cols, tile_count, tiles, omega)
    got = lax.ppermute(other, "samp", swap)
    mine = forward_near(near, held, table)
    own, *sends = pair_sum(mine, got)
    held, _ = lax.optimization_barrier((held, own))
    turned = turn(far, near, held)
    parts = [lax.ppermute(s, "samp", pairs(r)) for r, s in enumerate(sends)]
    own, turned = lax.optimization_barrier((own, turned))
    chunk = chunk_sum([own, *parts])
    pieces = [lax.ppermute(chunk, "samp", pairs(r)) for r in range(7)]
    own_half = gather_half(chunk, pieces)
    other_half = lax.ppermute(own_half, "samp", swap)
    first = backward_near(near, turned, own_half)
    keep, *shares, sketch = backward_far(far, turned, first, own_half, other_half)
    got = [line_permute(s, r, True) for r, s in enumerate(shares)]
    keep, *shares = line_sum(keep, got)
    got = [line_permute(s, r, False) for r, s in enumerate(shares)]
    factor = 1.0 / (KB_DEV * TILE * kmers) ** 0.5
    return sketch, last_sum(factor, keep, got)


def solution(mesh):
    placed = (
        P(("kmer", "samp"), None, None),
        P("samp", None),
        P(("kmer", "samp")),
        P(("kmer", "samp")),
        P(("kmer", "samp")),
    )
    return jax.shard_map(
        shards,
        mesh=mesh,
        in_specs=placed,
        out_specs=(P(("kmer", "samp"), None), P(("samp", "kmer"), None)),
        check_vma=False,
    )
```

```python
import functools

import jax
import jax.numpy as jnp
from jax import lax
from jax.experimental import pallas as pl
from jax.experimental.pallas import tpu as pltpu
from jax.sharding import PartitionSpec as P

TILE = 128
KB_DEV = 56
SB_DEV = 8
HALF_BLOCKS = KB_DEV // 2
HALF = HALF_BLOCKS * TILE
CHUNK_BLOCKS = KB_DEV // 8
CHUNK = CHUNK_BLOCKS * TILE
UNROLL = 12
LIST = 128
VMEM_LIMIT = 48 * 1024 * 1024

ROUNDS = (
    ((2, 0), (2, 1)),
    ((1, 0), (3, 1)),
    ((3, 0), (1, 1)),
    ((0, 1), (0, 0)),
)
BACK = (0, 2, 1, 3)

LINE = ((2, 2), (1, 3), (3, 1))


def vm():
    return pl.BlockSpec(memory_space=pltpu.VMEM)


def sm():
    return pl.BlockSpec(memory_space=pltpu.SMEM)


def params():
    return pltpu.CompilerParams(vmem_limit_bytes=VMEM_LIMIT)


def place():
    j = lax.axis_index("samp")
    return j // 8, (j // 2) % 4, j % 2


def pairs(r):
    out = []
    for s in range(16):
        z, x, c = s // 8, (s // 2) % 4, s % 2
        dx, dz = ROUNDS[r][c]
        out.append((s, (z ^ dz) * 8 + ((x + dx) % 4) * 2 + c))
    return out


def block(i):
    return pl.ds(pl.multiple_of(i * TILE, TILE), TILE)


def unpack(word):
    return lax.rem(word, 128), lax.rem(lax.div(word, 128), 64), lax.div(word, 8192)


def list_slots(rows, cols, count, far, near, shift, owner):
    cap = rows.shape[0]
    z, x, c = place()
    for m in range(8):
        dx = lax.rem(m % 4 + 4 - x, 4)
        same_z = z == m // 4
        for_core0 = jnp.where(dx == 0, jnp.logical_not(same_z), same_z)
        core = 1 - for_core0.astype(jnp.int32)
        d = jnp.where(core == 0, dx, lax.rem(4 - dx, 4))
        q = jnp.where(d == 0, 3, jnp.where(d == 2, 0, jnp.where(d == 1, 1, 2)))
        shift[m] = (q - m) * CHUNK_BLOCKS
        owner[m] = (core == c).astype(jnp.int32)

    def visit(s, carry):
        n_far, n_near = carry
        row = rows[s]
        m = (row * 37) >> 8
        word = s + (row + shift[m]) * 128 + cols[s] * 8192
        far[n_far] = word
        near[n_near] = word
        used = (s < count).astype(jnp.int32)
        here = used * owner[m]
        return n_far + used - here, n_near + here

    n_far, n_near = lax.fori_loop(0, cap, visit, (jnp.int32(0), jnp.int32(0)), unroll=8)
    pad = HALF_BLOCKS * 128 + SB_DEV * 8192
    pad_far, pad_near = pad + lax.rem(far[0], 128), pad + lax.rem(near[0], 128)
    for u in range(UNROLL):
        far[n_far + u] = pad_far
        near[n_near + u] = pad_near
    far[LIST - 1] = n_far
    near[LIST - 1] = n_near
    return n_far, n_near


def forward_slots(n, entries, tiles, omega, acc, out):
    acc[...] = jnp.zeros_like(acc)

    def step(g, carry):
        prods, where = [], []
        for u in range(UNROLL):
            slot, row, col = unpack(entries[g * UNROLL + u])
            col = jnp.minimum(col, SB_DEV - 1)
            where.append(block(row))
            prods.append(
                jnp.dot(tiles[slot], omega[block(col), :], preferred_element_type=jnp.float32)
            )
        for at, prod in zip(where, prods):
            acc[at, :] = acc[at, :] + prod
        return carry

    lax.fori_loop(0, (n + UNROLL - 1) // UNROLL, step, 0)
    out[...] = acc[pl.ds(0, HALF), :].astype(jnp.bfloat16)


def forward_far_kernel(
    rows, cols, count, tiles, omega, out, held, table, far, near, acc, s_rows, s_cols, shift, owner, sems
):
    small = [
        pltpu.make_async_copy(rows, s_rows, sems.at[0]),
        pltpu.make_async_copy(cols, s_cols, sems.at[1]),
    ]
    for copy in small:
        copy.start()
    fetch_omega = pltpu.make_async_copy(omega, table, sems.at[2])
    fetch_omega.start()
    for copy in small:
        copy.wait()
    n_far, n_near = list_slots(s_rows, s_cols, count[0], far, near, shift, owner)

    def fetch(entries, sem, k):
        slot = lax.rem(entries[k], 128)
        return pltpu.make_async_copy(tiles.at[slot], held.at[slot], sem)

    def start(entries, sem, n):
        def one(k, carry):
            fetch(entries, sem, k).start()
            return carry

        lax.fori_loop(0, n, one, 0)

    def wait(entries, sem, n):
        def one(k, carry):
            fetch(entries, sem, k).wait()
            return carry

        lax.fori_loop(0, n, one, 0)

    start(far, sems.at[3], n_far)
    start(near, sems.at[4], n_near)
    fetch_omega.wait()
    wait(far, sems.at[3], n_far)
    forward_slots(n_far, far, held, table, acc, out)
    wait(near, sems.at[4], n_near)


def forward_far(rows, cols, count, tiles, omega):
    cap = tiles.shape[0]
    anywhere = pl.BlockSpec(memory_space=pltpu.HBM)
    entries = jax.ShapeDtypeStruct((LIST,), jnp.int32)
    return pl.pallas_call(
        forward_far_kernel,
        out_shape=[
            jax.ShapeDtypeStruct((HALF, TILE), jnp.bfloat16),
            jax.ShapeDtypeStruct(tiles.shape, tiles.dtype),
            jax.ShapeDtypeStruct(omega.shape, omega.dtype),
            entries,
            entries,
        ],
        in_specs=[anywhere, anywhere, sm(), anywhere, anywhere],
        out_specs=[vm(), vm(), vm(), sm(), sm()],
        scratch_shapes=[
            pltpu.VMEM((HALF + TILE, TILE), jnp.float32),
            pltpu.SMEM((cap,), jnp.int32),
            pltpu.SMEM((cap,), jnp.int32),
            pltpu.SMEM((8,), jnp.int32),
            pltpu.SMEM((8,), jnp.int32),
            pltpu.SemaphoreType.DMA((5,)),
        ],
        compiler_params=params(),
        name="forward_far",
    )(*(pltpu.with_memory_space_constraint(v, pltpu.HBM) for v in (rows, cols)), count,
      *(pltpu.with_memory_space_constraint(v, pltpu.HBM) for v in (tiles, omega)))


def forward_near_kernel(near, held, table, out, acc):
    forward_slots(near[LIST - 1], near, held, table, acc, out)


def forward_near(near, held, table):
    return pl.pallas_call(
        forward_near_kernel,
        out_shape=jax.ShapeDtypeStruct((HALF, TILE), jnp.bfloat16),
        in_specs=[sm(), vm(), vm()],
        out_specs=vm(),
        scratch_shapes=[pltpu.VMEM((HALF + TILE, TILE), jnp.float32)],
        compiler_params=params(),
        name="forward_near",
    )(near, held, table)


def turn_kernel(far, near, tiles, out):
    def one(g, carry):
        for u in range(4):
            out[g * 4 + u] = tiles[g * 4 + u].T
        return carry

    lax.fori_loop(0, (far[LIST - 1] + near[LIST - 1] + 3) // 4, one, 0)


def turn(far, near, tiles):
    return pl.pallas_call(
        turn_kernel,
        out_shape=jax.ShapeDtypeStruct(tiles.shape, tiles.dtype),
        in_specs=[sm(), sm(), vm()],
        out_specs=vm(),
        compiler_params=params(),
        name="turn_tiles",
    )(far, near, tiles)


def chunk_at(q):
    return pl.ds(q * CHUNK, CHUNK)


def pair_kernel(a, b, *sends):
    for q, send in enumerate(sends):
        at = chunk_at(q)
        send[...] = (a[at, :].astype(jnp.float32) + b[at, :].astype(jnp.float32)).astype(jnp.bfloat16)


def pair_sum(a, b):
    shape = jax.ShapeDtypeStruct((CHUNK, TILE), jnp.bfloat16)
    return pl.pallas_call(
        pair_kernel,
        out_shape=[shape] * 4,
        in_specs=[vm(), vm()],
        out_specs=[vm()] * 4,
        compiler_params=params(),
        name="pair_sum",
    )(a, b)


def part_kernel(*refs):
    out = refs[-1]
    total = refs[0][...].astype(jnp.float32)
    for ref in refs[1:-1]:
        total = total + ref[...].astype(jnp.float32)
    out[...] = total.astype(jnp.bfloat16)


def part_sum(parts):
    return pl.pallas_call(
        part_kernel,
        out_shape=jax.ShapeDtypeStruct((CHUNK, TILE), jnp.bfloat16),
        in_specs=[vm()] * len(parts),
        out_specs=vm(),
        compiler_params=params(),
        name="part_sum",
    )(*parts)


def chunk_kernel(mine, got, out, sketch):
    out[...] = (mine[...].astype(jnp.float32) + got[...].astype(jnp.float32)).astype(jnp.bfloat16)
    _, _, c = place()
    size = sketch.shape[0]
    sketch[...] = out[pl.ds(pl.multiple_of(c * size, size), size), :]


def chunk_sum(mine, got):
    return pl.pallas_call(
        chunk_kernel,
        out_shape=[
            jax.ShapeDtypeStruct((CHUNK, TILE), jnp.bfloat16),
            jax.ShapeDtypeStruct((CHUNK // 2, TILE), jnp.bfloat16),
        ],
        in_specs=[vm(), vm()],
        out_specs=[vm(), vm()],
        compiler_params=params(),
        name="chunk_sum",
    )(mine, got)


def gather_kernel(*refs):
    for q in range(4):
        refs[-1][chunk_at(q), :] = refs[BACK[q]][...]


def gather_half(got):
    return pl.pallas_call(
        gather_kernel,
        out_shape=jax.ShapeDtypeStruct((HALF, TILE), jnp.bfloat16),
        in_specs=[vm()] * 4,
        out_specs=vm(),
        compiler_params=params(),
        name="gather_half",
    )(*got)


def backward_slots(n, entries, turned, table, acc):
    def step(g, carry):
        prods, where = [], []
        for u in range(UNROLL):
            slot, row, col = unpack(entries[g * UNROLL + u])
            row = jnp.minimum(row, HALF_BLOCKS - 1)
            where.append(block(col))
            prods.append(
                jnp.dot(turned[slot], table[block(row), :], preferred_element_type=jnp.float32)
            )
        for at, prod in zip(where, prods):
            acc[at, :] = acc[at, :] + prod
        return carry

    lax.fori_loop(0, (n + UNROLL - 1) // UNROLL, step, 0)


def backward_near_kernel(near, turned, table, out):
    out[...] = jnp.zeros_like(out)
    backward_slots(near[LIST - 1], near, turned, table, out)


def backward_near(near, turned, table):
    return pl.pallas_call(
        backward_near_kernel,
        out_shape=jax.ShapeDtypeStruct(((SB_DEV + 1) * TILE, TILE), jnp.float32),
        in_specs=[sm(), vm(), vm()],
        out_specs=vm(),
        compiler_params=params(),
        name="backward_near",
    )(near, turned, table)


def line_offset(r):
    _, _, c = place()
    return jnp.where(c == 0, LINE[r][0], LINE[r][1])


def share_at(i, size):
    return pl.ds(pl.multiple_of(lax.rem(i + 4, 4) * size, size), size)


def kmer_place():
    i = lax.axis_index("kmer")
    return i // 4, i % 4


def backward_far_kernel(far, turned, first, table, keep, s0, s1, s2, acc):
    acc[...] = first[...]
    backward_slots(far[LIST - 1], far, turned, table, acc)
    y, _ = kmer_place()
    size = keep.shape[0]
    for r, send in enumerate((s0, s1, s2)):
        send[...] = acc[share_at(y + line_offset(r), size), :].astype(jnp.bfloat16)
    keep[...] = acc[share_at(y, size), :]


def backward_far(far, turned, first, table):
    share = SB_DEV * TILE // 4
    send = jax.ShapeDtypeStruct((share, TILE), jnp.bfloat16)
    return pl.pallas_call(
        backward_far_kernel,
        out_shape=[jax.ShapeDtypeStruct((share, TILE), jnp.float32), send, send, send],
        in_specs=[sm(), vm(), vm(), vm()],
        out_specs=[vm()] * 4,
        scratch_shapes=[pltpu.VMEM(((SB_DEV + 1) * TILE, TILE), jnp.float32)],
        compiler_params=params(),
        name="backward_far",
    )(far, turned, first, table)


def line_kernel(own, g0, g1, g2, keep, send, acc):
    total = own[...]
    for got in (g0, g1, g2):
        total = total + got[...].astype(jnp.float32)
    acc[...] = total
    _, zh = kmer_place()
    size = keep.shape[0] // 2
    peer = zh + 1 - 2 * lax.rem(zh, 2)
    for k, (mine, theirs) in enumerate(((zh, peer), (3 - zh, 3 - peer))):
        keep[pl.ds(k * size, size), :] = acc[share_at(mine, size), :]
        send[pl.ds(k * size, size), :] = acc[share_at(theirs, size), :].astype(jnp.bfloat16)


def line_sum(own, got):
    half = own.shape[0] // 2
    return pl.pallas_call(
        line_kernel,
        out_shape=[
            jax.ShapeDtypeStruct((half, TILE), jnp.float32),
            jax.ShapeDtypeStruct((half, TILE), jnp.bfloat16),
        ],
        in_specs=[vm()] * 4,
        out_specs=[vm()] * 2,
        scratch_shapes=[pltpu.VMEM(own.shape, jnp.float32)],
        compiler_params=params(),
        name="line_sum",
    )(own, *got)


def halve_kernel(own, got, keep, send):
    size = keep.shape[0]
    total = own[...] + got[...].astype(jnp.float32)
    keep[...] = total[:size]
    send[...] = total[size:].astype(jnp.bfloat16)


def halve_sum(own, got):
    half = own.shape[0] // 2
    return pl.pallas_call(
        halve_kernel,
        out_shape=[
            jax.ShapeDtypeStruct((half, TILE), jnp.float32),
            jax.ShapeDtypeStruct((half, TILE), jnp.bfloat16),
        ],
        in_specs=[vm()] * 2,
        out_specs=[vm()] * 2,
        compiler_params=params(),
        name="halve_sum",
    )(own, got)


def last_kernel(factor, own, got, out):
    out[...] = (own[...] + got[...].astype(jnp.float32)) * factor


def last_sum(factor, own, got):
    return pl.pallas_call(
        functools.partial(last_kernel, factor),
        out_shape=jax.ShapeDtypeStruct(own.shape, jnp.float32),
        in_specs=[vm()] * 2,
        out_specs=vm(),
        compiler_params=params(),
        name="last_sum",
    )(own, got)


def y_pairs(r):
    out = []
    for i in range(16):
        for j in range(16):
            to = ((i // 4 + LINE[r][j % 2]) % 4) * 4 + i % 4
            out.append((i * 16 + j, to * 16 + j))
    return out


def shards(tiles, omega, tile_rows, tile_cols, tile_count):
    swap = [(s, s ^ 1) for s in range(16)]
    kmers = lax.axis_size("kmer")
    other, held, table, far, near = forward_far(tile_rows, tile_cols, tile_count, tiles, omega)
    got = lax.ppermute(other, "samp", swap)
    mine = forward_near(near, held, table)
    sends = pair_sum(mine, got)
    held, *_ = lax.optimization_barrier((held, *sends))
    turned = turn(far, near, held)
    parts = [lax.ppermute(s, "samp", pairs(r)) for r, s in enumerate(sends)]
    *parts, turned = lax.optimization_barrier((*parts, turned))
    part = part_sum(parts)
    chunk, sketch = chunk_sum(part, lax.ppermute(part, "samp", swap))
    half = gather_half([lax.ppermute(chunk, "samp", pairs(r)) for r in (3, 2, 1, 0)][::-1])
    rest = lax.ppermute(half, "samp", swap)
    first = backward_near(near, turned, half)
    keep, *shares = backward_far(far, turned, first, rest)
    got = [lax.ppermute(s, ("kmer", "samp"), y_pairs(r)) for r, s in enumerate(shares)]
    keep, share = line_sum(keep, got)
    keep, share = halve_sum(keep, lax.ppermute(share, "kmer", [(i, i ^ 1) for i in range(16)]))
    got = lax.ppermute(share, "kmer", [(i, i // 4 * 4 + 3 - i % 4) for i in range(16)])
    factor = 1.0 / (KB_DEV * TILE * kmers) ** 0.5
    return sketch, last_sum(factor, keep, got)


def solution(mesh):
    placed = (
        P(("kmer", "samp"), None, None),
        P("samp", None),
        P(("kmer", "samp")),
        P(("kmer", "samp")),
        P(("kmer", "samp")),
    )
    return jax.shard_map(
        shards,
        mesh=mesh,
        in_specs=placed,
        out_specs=(P(("kmer", "samp"), None), P(("samp", "kmer"), None)),
        check_vma=False,
    )
```

```python
import functools

import jax
import jax.numpy as jnp
from jax import lax
from jax.experimental import pallas as pl
from jax.experimental.pallas import tpu as pltpu
from jax.sharding import PartitionSpec as P

TILE = 128
KB_DEV = 56
SB_DEV = 8
CHUNK_BLOCKS = KB_DEV // 8
CHUNK = CHUNK_BLOCKS * TILE
PART_BLOCKS = 2 * CHUNK_BLOCKS
PART = PART_BLOCKS * TILE
UNROLL = 12
LIST = 128
FETCH = 8
VMEM_LIMIT = 48 * 1024 * 1024
COST = pl.CostEstimate(flops=200 * 44 * TILE**3, bytes_accessed=200 * 44 * TILE**2, transcendentals=0)

ROUNDS = (
    ((1, 0), (3, 1)),
    ((3, 0), (1, 1)),
    ((2, 0), (2, 1)),
    ((0, 1), (0, 0)),
)
NEAR_EARLY, NEAR_LATE, FAR_EARLY, FAR_LATE = range(4)
LINE = ((2, 2), (1, 3), (3, 1))


def vm():
    return pl.BlockSpec(memory_space=pltpu.VMEM)


def sm():
    return pl.BlockSpec(memory_space=pltpu.SMEM)


def params():
    return pltpu.CompilerParams(vmem_limit_bytes=VMEM_LIMIT)


def place():
    j = lax.axis_index("samp")
    return j // 8, (j // 2) % 4, j % 2


def kmer_place():
    i = lax.axis_index("kmer")
    return i // 4, i % 4


def round_pairs(p):
    out = []
    for s in range(16):
        z, x, c = s // 8, (s // 2) % 4, s % 2
        dx, dz = ROUNDS[p][c]
        out.append((s, (z ^ dz) * 8 + (x ^ dx) * 2 + c))
    return out


def y_pairs(r):
    out = []
    for i in range(16):
        for j in range(16):
            to = ((i // 4 + LINE[r][j % 2]) % 4) * 4 + i % 4
            out.append((i * 16 + j, to * 16 + j))
    return out


def block(i):
    return pl.ds(pl.multiple_of(i * TILE, TILE), TILE)


def chunk_at(q):
    return pl.ds(q * CHUNK, CHUNK)


def unpack(word):
    return lax.rem(word, 128), lax.rem(lax.div(word, 128), 64), lax.div(word, 8192)


def size_of(lists, which):
    return lists[which * LIST + LIST - 1]


def list_slots(rows, cols, count, lists, shift, owner):
    cap = rows.shape[0]
    z, x, c = place()
    for m in range(8):
        mx = m % 4
        e = jnp.bitwise_xor(x, mx)
        same_z = (z == m // 4).astype(jnp.int32)
        core = jnp.where(e == 0, same_z, 1 - same_z)
        odd = jnp.where(core == 0, e == 3, e == 1).astype(jnp.int32)
        p = jnp.where(e == 0, 3, jnp.where(e == 2, 2, odd))
        late = (p >= 2).astype(jnp.int32)
        shift[m] = (p - 2 * late - m) * CHUNK_BLOCKS
        owner[m] = jnp.where(core == c, 0, 2) + late

    def visit(s, sizes):
        row = rows[s]
        m = (row * 37) >> 8
        word = s + (row + shift[m]) * 128 + cols[s] * 8192
        which = jnp.where(s < count, owner[m], 4)
        for k, n in enumerate(sizes):
            lists[k * LIST + n] = word
        return tuple(n + (which == k).astype(jnp.int32) for k, n in enumerate(sizes))

    sizes = lax.fori_loop(0, cap, visit, (jnp.int32(0),) * 4, unroll=8)
    for k, n in enumerate(sizes):
        pad = lax.rem(lists[k * LIST], 128) + PART_BLOCKS * 128 + SB_DEV * 8192
        for u in range(UNROLL):
            lists[k * LIST + n + u] = pad
        lists[k * LIST + LIST - 1] = n


def forward_slots(lists, which, tiles, omega, acc, out):
    acc[...] = jnp.zeros_like(acc)

    def step(g, carry):
        prods, where = [], []
        for u in range(UNROLL):
            slot, row, col = unpack(lists[which * LIST + g * UNROLL + u])
            col = jnp.minimum(col, SB_DEV - 1)
            where.append(block(row))
            prods.append(
                jnp.dot(tiles[slot], omega[block(col), :], preferred_element_type=jnp.float32)
            )
        for at, prod in zip(where, prods):
            acc[at, :] = acc[at, :] + prod
        return carry

    lax.fori_loop(0, (size_of(lists, which) + UNROLL - 1) // UNROLL, step, 0)
    out[...] = acc[pl.ds(0, PART), :].astype(jnp.bfloat16)


def forward_first_kernel(
    rows, cols, count, tiles, omega, out, held, table, lists, acc, s_rows, s_cols, shift, owner, sems, tile_sems
):
    small = [
        pltpu.make_async_copy(rows, s_rows, sems.at[0]),
        pltpu.make_async_copy(cols, s_cols, sems.at[1]),
    ]
    for copy in small:
        copy.start()
    used = count[0]

    def fetch(g):
        at = pl.ds(g * FETCH, FETCH)
        return pltpu.make_async_copy(tiles.at[at], held.at[at], tile_sems.at[g])

    fetches = tiles.shape[0] // FETCH
    for g in range(fetches):
        pl.when(g * FETCH < used)(fetch(g).start)
    fetch_omega = pltpu.make_async_copy(omega, table, sems.at[2])
    fetch_omega.start()
    for copy in small:
        copy.wait()
    list_slots(s_rows, s_cols, used, lists, shift, owner)
    for g in range(fetches):
        pl.when(g * FETCH < used)(fetch(g).wait)
    fetch_omega.wait()
    forward_slots(lists, FAR_EARLY, held, table, acc, out)


def in_hbm(value):
    return pltpu.with_memory_space_constraint(value, pltpu.HBM)


def forward_first(rows, cols, count, tiles, omega):
    cap = tiles.shape[0]
    anywhere = pl.BlockSpec(memory_space=pltpu.HBM)
    return pl.pallas_call(
        forward_first_kernel,
        out_shape=[
            jax.ShapeDtypeStruct((PART, TILE), jnp.bfloat16),
            jax.ShapeDtypeStruct(tiles.shape, tiles.dtype),
            jax.ShapeDtypeStruct(omega.shape, omega.dtype),
            jax.ShapeDtypeStruct((4 * LIST,), jnp.int32),
        ],
        in_specs=[anywhere, anywhere, sm(), anywhere, anywhere],
        out_specs=[vm(), vm(), vm(), sm()],
        scratch_shapes=[
            pltpu.VMEM((PART + TILE, TILE), jnp.float32),
            pltpu.SMEM((cap,), jnp.int32),
            pltpu.SMEM((cap,), jnp.int32),
            pltpu.SMEM((8,), jnp.int32),
            pltpu.SMEM((8,), jnp.int32),
            pltpu.SemaphoreType.DMA((3,)),
            pltpu.SemaphoreType.DMA((cap // FETCH,)),
        ],
        compiler_params=params(),
        name="forward_first",
    )(in_hbm(rows), in_hbm(cols), count, in_hbm(tiles), in_hbm(omega))


def forward_next_kernel(which, lists, held, table, out, acc):
    forward_slots(lists, which, held, table, acc, out)


def forward_next(which, lists, held, table):
    return pl.pallas_call(
        functools.partial(forward_next_kernel, which),
        out_shape=jax.ShapeDtypeStruct((PART, TILE), jnp.bfloat16),
        in_specs=[sm(), vm(), vm()],
        out_specs=vm(),
        scratch_shapes=[pltpu.VMEM((PART + TILE, TILE), jnp.float32)],
        compiler_params=params(),
        cost_estimate=COST,
        name=f"forward_next{which}",
    )(lists, held, table)


def turn_kernel(count, tiles, out):
    def one(g, carry):
        for u in range(4):
            out[g * 4 + u] = tiles[g * 4 + u].T
        return carry

    lax.fori_loop(0, (count[0] + 3) // 4, one, 0)


def turn(count, tiles):
    return pl.pallas_call(
        turn_kernel,
        out_shape=jax.ShapeDtypeStruct(tiles.shape, tiles.dtype),
        in_specs=[sm(), vm()],
        out_specs=vm(),
        compiler_params=params(),
        name="turn_tiles",
    )(count, tiles)


def pair_kernel(a, b, *sends):
    for q, send in enumerate(sends):
        at = chunk_at(q)
        send[...] = (a[at, :].astype(jnp.float32) + b[at, :].astype(jnp.float32)).astype(jnp.bfloat16)


def pair_sum(a, b):
    shape = jax.ShapeDtypeStruct((CHUNK, TILE), jnp.bfloat16)
    return pl.pallas_call(
        pair_kernel,
        out_shape=[shape] * 2,
        in_specs=[vm(), vm()],
        out_specs=[vm()] * 2,
        compiler_params=params(),
        name="pair_sum",
    )(a, b)


def part_kernel(*refs):
    out = refs[-1]
    total = refs[0][...].astype(jnp.float32)
    for ref in refs[1:-1]:
        total = total + ref[...].astype(jnp.float32)
    out[...] = total.astype(jnp.bfloat16)


def part_sum(name, *parts):
    return pl.pallas_call(
        part_kernel,
        out_shape=jax.ShapeDtypeStruct((CHUNK, TILE), jnp.bfloat16),
        in_specs=[vm()] * len(parts),
        out_specs=vm(),
        compiler_params=params(),
        name=name,
    )(*parts)


def backward_slots(lists, which, turned, table, acc):
    def step(g, carry):
        prods, where = [], []
        for u in range(UNROLL):
            slot, row, col = unpack(lists[which * LIST + g * UNROLL + u])
            row = jnp.minimum(row, PART_BLOCKS - 1)
            where.append(block(col))
            prods.append(
                jnp.dot(turned[slot], table[block(row), :], preferred_element_type=jnp.float32)
            )
        for at, prod in zip(where, prods):
            acc[at, :] = acc[at, :] + prod
        return carry

    lax.fori_loop(0, (size_of(lists, which) + UNROLL - 1) // UNROLL, step, 0)


def backward_part(lists, kinds, turned, near, far, table, acc):
    for kind, pieces in zip(kinds, (near, far)):
        for q, piece in enumerate(pieces):
            table[chunk_at(q), :] = piece[...]
        backward_slots(lists, kind, turned, table, acc)


def backward_early_kernel(lists, turned, chunk, n0, n1, f0, f1, out, sketch, table):
    out[...] = jnp.zeros_like(out)
    backward_part(lists, (NEAR_EARLY, FAR_EARLY), turned, (n0, n1), (f0, f1), table, out)
    _, _, c = place()
    size = sketch.shape[0]
    sketch[...] = chunk[pl.ds(pl.multiple_of(c * size, size), size), :]


def backward_early(lists, turned, chunk, near, far):
    return pl.pallas_call(
        backward_early_kernel,
        out_shape=[
            jax.ShapeDtypeStruct(((SB_DEV + 1) * TILE, TILE), jnp.float32),
            jax.ShapeDtypeStruct((CHUNK // 2, TILE), jnp.bfloat16),
        ],
        in_specs=[sm()] + [vm()] * 6,
        out_specs=[vm()] * 2,
        scratch_shapes=[pltpu.VMEM((PART, TILE), jnp.bfloat16)],
        compiler_params=params(),
        cost_estimate=COST,
        name="backward_early",
    )(lists, turned, chunk, *near, *far)


def line_offset(r):
    _, _, c = place()
    return jnp.where(c == 0, LINE[r][0], LINE[r][1])


def share_at(i, size):
    return pl.ds(pl.multiple_of(lax.rem(i + 4, 4) * size, size), size)


def backward_late_kernel(lists, turned, first, n2, n3, f2, f3, keep, s0, s1, s2, acc, table):
    acc[...] = first[...]
    backward_part(lists, (NEAR_LATE, FAR_LATE), turned, (n2, n3), (f2, f3), table, acc)
    y, _ = kmer_place()
    size = keep.shape[0]
    for r, send in enumerate((s0, s1, s2)):
        send[...] = acc[share_at(y + line_offset(r), size), :].astype(jnp.bfloat16)
    keep[...] = acc[share_at(y, size), :]


def backward_late(lists, turned, first, near, far):
    share = SB_DEV * TILE // 4
    send = jax.ShapeDtypeStruct((share, TILE), jnp.bfloat16)
    return pl.pallas_call(
        backward_late_kernel,
        out_shape=[jax.ShapeDtypeStruct((share, TILE), jnp.float32), send, send, send],
        in_specs=[sm()] + [vm()] * 6,
        out_specs=[vm()] * 4,
        scratch_shapes=[
            pltpu.VMEM(((SB_DEV + 1) * TILE, TILE), jnp.float32),
            pltpu.VMEM((PART, TILE), jnp.bfloat16),
        ],
        compiler_params=params(),
        name="backward_late",
    )(lists, turned, first, *near, *far)


def line_kernel(own, g0, g1, g2, keep, send, acc):
    total = own[...]
    for got in (g0, g1, g2):
        total = total + got[...].astype(jnp.float32)
    acc[...] = total
    _, zh = kmer_place()
    size = keep.shape[0] // 2
    peer = zh + 1 - 2 * lax.rem(zh, 2)
    for k, (mine, theirs) in enumerate(((zh, peer), (3 - zh, 3 - peer))):
        keep[pl.ds(k * size, size), :] = acc[share_at(mine, size), :]
        send[pl.ds(k * size, size), :] = acc[share_at(theirs, size), :].astype(jnp.bfloat16)


def line_sum(own, got):
    half = own.shape[0] // 2
    return pl.pallas_call(
        line_kernel,
        out_shape=[
            jax.ShapeDtypeStruct((half, TILE), jnp.float32),
            jax.ShapeDtypeStruct((half, TILE), jnp.bfloat16),
        ],
        in_specs=[vm()] * 4,
        out_specs=[vm()] * 2,
        scratch_shapes=[pltpu.VMEM(own.shape, jnp.float32)],
        compiler_params=params(),
        name="line_sum",
    )(own, *got)


def halve_kernel(own, got, keep, send):
    size = keep.shape[0]
    total = own[...] + got[...].astype(jnp.float32)
    keep[...] = total[:size]
    send[...] = total[size:].astype(jnp.bfloat16)


def halve_sum(own, got):
    half = own.shape[0] // 2
    return pl.pallas_call(
        halve_kernel,
        out_shape=[
            jax.ShapeDtypeStruct((half, TILE), jnp.float32),
            jax.ShapeDtypeStruct((half, TILE), jnp.bfloat16),
        ],
        in_specs=[vm()] * 2,
        out_specs=[vm()] * 2,
        compiler_params=params(),
        name="halve_sum",
    )(own, got)


def last_kernel(factor, own, got, out):
    out[...] = (own[...] + got[...].astype(jnp.float32)) * factor


def last_sum(factor, own, got):
    return pl.pallas_call(
        functools.partial(last_kernel, factor),
        out_shape=jax.ShapeDtypeStruct(own.shape, jnp.float32),
        in_specs=[vm()] * 2,
        out_specs=vm(),
        compiler_params=params(),
        name="last_sum",
    )(own, got)


def swap(value):
    return lax.ppermute(value, "samp", [(s, s ^ 1) for s in range(16)])


def trade(value, p):
    return lax.ppermute(value, "samp", round_pairs(p))


def after(value, *first):
    return lax.optimization_barrier((value, *first))[0]


def shards(tiles, omega, tile_rows, tile_cols, tile_count):
    kmers = lax.axis_size("kmer")
    other, held, table, lists = forward_first(tile_rows, tile_cols, tile_count, tiles, omega)
    sends = pair_sum(forward_next(NEAR_EARLY, lists, held, table), swap(other))
    held_late = after(held, *sends)
    parts = [trade(s, p) for p, s in enumerate(sends)]
    other = forward_next(FAR_LATE, lists, held_late, table)
    sends = pair_sum(forward_next(NEAR_LATE, lists, held_late, table), swap(other))
    parts += [trade(s, p + 2) for p, s in enumerate(sends)]
    turned = turn(tile_count, after(held, *sends))
    part = part_sum("part_sum", *parts)
    part, turned = lax.optimization_barrier((part, turned))
    chunk = part_sum("chunk_sum", part, swap(part))
    near = [trade(chunk, p) for p in range(4)]
    far = [swap(piece) for piece in near]
    first, sketch = backward_early(lists, turned, chunk, near[:2], far[:2])
    keep, *shares = backward_late(lists, turned, first, near[2:], far[2:])
    got = [lax.ppermute(s, ("kmer", "samp"), y_pairs(r)) for r, s in enumerate(shares)]
    keep, share = line_sum(keep, got)
    keep, share = halve_sum(keep, lax.ppermute(share, "kmer", [(i, i ^ 1) for i in range(16)]))
    got = lax.ppermute(share, "kmer", [(i, i // 4 * 4 + 3 - i % 4) for i in range(16)])
    factor = 1.0 / (KB_DEV * TILE * kmers) ** 0.5
    return sketch, last_sum(factor, keep, got)


def solution(mesh):
    placed = (
        P(("kmer", "samp"), None, None),
        P("samp", None),
        P(("kmer", "samp")),
        P(("kmer", "samp")),
        P(("kmer", "samp")),
    )
    return jax.shard_map(
        shards,
        mesh=mesh,
        in_specs=placed,
        out_specs=(P(("kmer", "samp"), None), P(("samp", "kmer"), None)),
        check_vma=False,
    )
```

```python
import functools

import jax
import jax.numpy as jnp
from jax import lax
from jax.experimental import pallas as pl
from jax.experimental.pallas import tpu as pltpu
from jax.sharding import PartitionSpec as P

TILE = 128
KB_DEV = 56
SB_DEV = 8
CHUNK_BLOCKS = KB_DEV // 8
CHUNK = CHUNK_BLOCKS * TILE
PART_BLOCKS = 2 * CHUNK_BLOCKS
PART = PART_BLOCKS * TILE
UNROLL = 12
LIST = 128
FETCH = 8
VMEM_LIMIT = 48 * 1024 * 1024
COST = pl.CostEstimate(flops=200 * 44 * TILE**3, bytes_accessed=200 * 44 * TILE**2, transcendentals=0)

ROUNDS = (
    ((1, 0), (3, 1)),
    ((3, 0), (1, 1)),
    ((2, 0), (2, 1)),
    ((0, 0), (0, 1)),
)
NEAR_EARLY, NEAR_LATE, FAR_EARLY, FAR_LATE = range(4)
LINE = ((2, 2), (1, 3), (3, 1))


def vm():
    return pl.BlockSpec(memory_space=pltpu.VMEM)


def sm():
    return pl.BlockSpec(memory_space=pltpu.SMEM)


def params():
    return pltpu.CompilerParams(vmem_limit_bytes=VMEM_LIMIT)


def place():
    j = lax.axis_index("samp")
    return j // 8, (j // 2) % 4, j % 2


def kmer_place():
    i = lax.axis_index("kmer")
    return i // 4, i % 4


def round_pairs(p):
    out = []
    for s in range(16):
        z, x, c = s // 8, (s // 2) % 4, s % 2
        dx, dz = ROUNDS[p][c]
        out.append((s, (z ^ dz) * 8 + (x ^ dx) * 2 + c))
    return out


def y_pairs(r):
    out = []
    for i in range(16):
        for j in range(16):
            to = ((i // 4 + LINE[r][j % 2]) % 4) * 4 + i % 4
            out.append((i * 16 + j, to * 16 + j))
    return out


def block(i):
    return pl.ds(pl.multiple_of(i * TILE, TILE), TILE)


def chunk_at(q):
    return pl.ds(q * CHUNK, CHUNK)


def unpack(word):
    return lax.rem(word, 128), lax.rem(lax.div(word, 128), 64), lax.div(word, 8192)


def size_of(lists, which):
    return lists[which * LIST + LIST - 1]


def list_slots(rows, cols, count, lists, shift, owner):
    cap = rows.shape[0]
    z, x, c = place()
    for m in range(8):
        mx = m % 4
        e = jnp.bitwise_xor(x, mx)
        same_z = (z == m // 4).astype(jnp.int32)
        core = 1 - same_z
        odd = jnp.where(core == 0, e == 3, e == 1).astype(jnp.int32)
        p = jnp.where(e == 0, 3, jnp.where(e == 2, 2, odd))
        late = (p >= 2).astype(jnp.int32)
        shift[m] = (p - 2 * late - m) * CHUNK_BLOCKS
        owner[m] = jnp.where(core == c, 0, 2) + late

    def visit(s, sizes):
        row = rows[s]
        m = (row * 37) >> 8
        word = s + (row + shift[m]) * 128 + cols[s] * 8192
        which = jnp.where(s < count, owner[m], 4)
        for k, n in enumerate(sizes):
            lists[k * LIST + n] = word
        return tuple(n + (which == k).astype(jnp.int32) for k, n in enumerate(sizes))

    sizes = lax.fori_loop(0, cap, visit, (jnp.int32(0),) * 4, unroll=8)
    for k, n in enumerate(sizes):
        pad = lax.rem(lists[k * LIST], 128) + PART_BLOCKS * 128 + SB_DEV * 8192
        for u in range(UNROLL):
            lists[k * LIST + n + u] = pad
        lists[k * LIST + LIST - 1] = n


def forward_slots(lists, which, tiles, omega, acc, out):
    acc[...] = jnp.zeros_like(acc)

    def step(g, carry):
        prods, where = [], []
        for u in range(UNROLL):
            slot, row, col = unpack(lists[which * LIST + g * UNROLL + u])
            col = jnp.minimum(col, SB_DEV - 1)
            where.append(block(row))
            prods.append(
                jnp.dot(tiles[slot], omega[block(col), :], preferred_element_type=jnp.float32)
            )
        for at, prod in zip(where, prods):
            acc[at, :] = acc[at, :] + prod
        return carry

    lax.fori_loop(0, (size_of(lists, which) + UNROLL - 1) // UNROLL, step, 0)
    out[...] = acc[pl.ds(0, PART), :].astype(jnp.bfloat16)


def forward_first_kernel(
    rows, cols, count, tiles, omega, out, held, table, lists, acc, s_rows, s_cols, shift, owner, sems, tile_sems
):
    small = [
        pltpu.make_async_copy(rows, s_rows, sems.at[0]),
        pltpu.make_async_copy(cols, s_cols, sems.at[1]),
    ]
    for copy in small:
        copy.start()
    used = count[0]

    def fetch(g):
        at = pl.ds(g * FETCH, FETCH)
        return pltpu.make_async_copy(tiles.at[at], held.at[at], tile_sems.at[g])

    fetches = tiles.shape[0] // FETCH
    for g in range(fetches):
        pl.when(g * FETCH < used)(fetch(g).start)
    fetch_omega = pltpu.make_async_copy(omega, table, sems.at[2])
    fetch_omega.start()
    for copy in small:
        copy.wait()
    list_slots(s_rows, s_cols, used, lists, shift, owner)
    for g in range(fetches):
        pl.when(g * FETCH < used)(fetch(g).wait)
    fetch_omega.wait()
    forward_slots(lists, FAR_EARLY, held, table, acc, out)


def in_hbm(value):
    return pltpu.with_memory_space_constraint(value, pltpu.HBM)


def forward_first(rows, cols, count, tiles, omega):
    cap = tiles.shape[0]
    anywhere = pl.BlockSpec(memory_space=pltpu.HBM)
    return pl.pallas_call(
        forward_first_kernel,
        out_shape=[
            jax.ShapeDtypeStruct((PART, TILE), jnp.bfloat16),
            jax.ShapeDtypeStruct(tiles.shape, tiles.dtype),
            jax.ShapeDtypeStruct(omega.shape, omega.dtype),
            jax.ShapeDtypeStruct((4 * LIST,), jnp.int32),
        ],
        in_specs=[anywhere, anywhere, sm(), anywhere, anywhere],
        out_specs=[vm(), vm(), vm(), sm()],
        scratch_shapes=[
            pltpu.VMEM((PART + TILE, TILE), jnp.float32),
            pltpu.SMEM((cap,), jnp.int32),
            pltpu.SMEM((cap,), jnp.int32),
            pltpu.SMEM((8,), jnp.int32),
            pltpu.SMEM((8,), jnp.int32),
            pltpu.SemaphoreType.DMA((3,)),
            pltpu.SemaphoreType.DMA((cap // FETCH,)),
        ],
        compiler_params=params(),
        name="forward_first",
    )(in_hbm(rows), in_hbm(cols), count, in_hbm(tiles), in_hbm(omega))


def forward_next_kernel(which, lists, held, table, out, acc):
    forward_slots(lists, which, held, table, acc, out)


def forward_next(which, lists, held, table):
    return pl.pallas_call(
        functools.partial(forward_next_kernel, which),
        out_shape=jax.ShapeDtypeStruct((PART, TILE), jnp.bfloat16),
        in_specs=[sm(), vm(), vm()],
        out_specs=vm(),
        scratch_shapes=[pltpu.VMEM((PART + TILE, TILE), jnp.float32)],
        compiler_params=params(),
        cost_estimate=COST,
        name=f"forward_next{which}",
    )(lists, held, table)


def turn_kernel(count, tiles, out):
    def one(g, carry):
        for u in range(4):
            out[g * 4 + u] = tiles[g * 4 + u].T
        return carry

    lax.fori_loop(0, (count[0] + 3) // 4, one, 0)


def turn(count, tiles):
    return pl.pallas_call(
        turn_kernel,
        out_shape=jax.ShapeDtypeStruct(tiles.shape, tiles.dtype),
        in_specs=[sm(), vm()],
        out_specs=vm(),
        compiler_params=params(),
        name="turn_tiles",
    )(count, tiles)


def pair_kernel(a, b, *sends):
    for q, send in enumerate(sends):
        at = chunk_at(q)
        send[...] = (a[at, :].astype(jnp.float32) + b[at, :].astype(jnp.float32)).astype(jnp.bfloat16)


def pair_sum(a, b):
    shape = jax.ShapeDtypeStruct((CHUNK, TILE), jnp.bfloat16)
    return pl.pallas_call(
        pair_kernel,
        out_shape=[shape] * 2,
        in_specs=[vm(), vm()],
        out_specs=[vm()] * 2,
        compiler_params=params(),
        name="pair_sum",
    )(a, b)


def part_kernel(*refs):
    out = refs[-1]
    total = refs[0][...].astype(jnp.float32)
    for ref in refs[1:-1]:
        total = total + ref[...].astype(jnp.float32)
    out[...] = total.astype(jnp.bfloat16)


def part_sum(name, *parts):
    return pl.pallas_call(
        part_kernel,
        out_shape=jax.ShapeDtypeStruct((CHUNK, TILE), jnp.bfloat16),
        in_specs=[vm()] * len(parts),
        out_specs=vm(),
        compiler_params=params(),
        name=name,
    )(*parts)


def backward_slots(lists, which, turned, table, acc):
    def step(g, carry):
        prods, where = [], []
        for u in range(UNROLL):
            slot, row, col = unpack(lists[which * LIST + g * UNROLL + u])
            row = jnp.minimum(row, PART_BLOCKS - 1)
            where.append(block(col))
            prods.append(
                jnp.dot(turned[slot], table[block(row), :], preferred_element_type=jnp.float32)
            )
        for at, prod in zip(where, prods):
            acc[at, :] = acc[at, :] + prod
        return carry

    lax.fori_loop(0, (size_of(lists, which) + UNROLL - 1) // UNROLL, step, 0)


def backward_part(lists, kinds, turned, near, far, table, acc):
    for kind, pieces in zip(kinds, (near, far)):
        for q, piece in enumerate(pieces):
            table[chunk_at(q), :] = piece[...]
        backward_slots(lists, kind, turned, table, acc)


def sketch_kernel(chunk, out):
    _, _, c = place()
    size = out.shape[0]
    out[...] = chunk[pl.ds(pl.multiple_of(c * size, size), size), :]


def sketch_rows(chunk):
    return pl.pallas_call(
        sketch_kernel,
        out_shape=jax.ShapeDtypeStruct((CHUNK // 2, TILE), jnp.bfloat16),
        in_specs=[vm()],
        out_specs=vm(),
        compiler_params=params(),
        name="sketch_rows",
    )(chunk)


def backward_early_kernel(lists, turned, n0, n1, f0, f1, out, table):
    out[...] = jnp.zeros_like(out)
    backward_part(lists, (NEAR_EARLY, FAR_EARLY), turned, (n0, n1), (f0, f1), table, out)


def backward_early(lists, turned, near, far):
    return pl.pallas_call(
        backward_early_kernel,
        out_shape=jax.ShapeDtypeStruct(((SB_DEV + 1) * TILE, TILE), jnp.float32),
        in_specs=[sm()] + [vm()] * 5,
        out_specs=vm(),
        scratch_shapes=[pltpu.VMEM((PART, TILE), jnp.bfloat16)],
        compiler_params=params(),
        cost_estimate=COST,
        name="backward_early",
    )(lists, turned, *near, *far)


def line_offset(r):
    _, _, c = place()
    return jnp.where(c == 0, LINE[r][0], LINE[r][1])


def share_at(i, size):
    return pl.ds(pl.multiple_of(lax.rem(i + 4, 4) * size, size), size)


def backward_late_kernel(lists, turned, first, n2, n3, f2, f3, keep, s0, s1, s2, acc, table):
    acc[...] = first[...]
    backward_part(lists, (NEAR_LATE, FAR_LATE), turned, (n2, n3), (f2, f3), table, acc)
    y, _ = kmer_place()
    size = keep.shape[0]
    for r, send in enumerate((s0, s1, s2)):
        send[...] = acc[share_at(y + line_offset(r), size), :].astype(jnp.bfloat16)
    keep[...] = acc[share_at(y, size), :]


def backward_late(lists, turned, first, near, far):
    share = SB_DEV * TILE // 4
    send = jax.ShapeDtypeStruct((share, TILE), jnp.bfloat16)
    return pl.pallas_call(
        backward_late_kernel,
        out_shape=[jax.ShapeDtypeStruct((share, TILE), jnp.float32), send, send, send],
        in_specs=[sm()] + [vm()] * 6,
        out_specs=[vm()] * 4,
        scratch_shapes=[
            pltpu.VMEM(((SB_DEV + 1) * TILE, TILE), jnp.float32),
            pltpu.VMEM((PART, TILE), jnp.bfloat16),
        ],
        compiler_params=params(),
        name="backward_late",
    )(lists, turned, first, *near, *far)


def line_kernel(own, g0, g1, g2, keep, send, acc):
    total = own[...]
    for got in (g0, g1, g2):
        total = total + got[...].astype(jnp.float32)
    acc[...] = total
    _, zh = kmer_place()
    size = keep.shape[0] // 2
    peer = zh + 1 - 2 * lax.rem(zh, 2)
    for k, (mine, theirs) in enumerate(((zh, peer), (3 - zh, 3 - peer))):
        keep[pl.ds(k * size, size), :] = acc[share_at(mine, size), :]
        send[pl.ds(k * size, size), :] = acc[share_at(theirs, size), :].astype(jnp.bfloat16)


def line_sum(own, got):
    half = own.shape[0] // 2
    return pl.pallas_call(
        line_kernel,
        out_shape=[
            jax.ShapeDtypeStruct((half, TILE), jnp.float32),
            jax.ShapeDtypeStruct((half, TILE), jnp.bfloat16),
        ],
        in_specs=[vm()] * 4,
        out_specs=[vm()] * 2,
        scratch_shapes=[pltpu.VMEM(own.shape, jnp.float32)],
        compiler_params=params(),
        name="line_sum",
    )(own, *got)


def halve_kernel(own, got, keep, send):
    size = keep.shape[0]
    total = own[...] + got[...].astype(jnp.float32)
    keep[...] = total[:size]
    send[...] = total[size:].astype(jnp.bfloat16)


def halve_sum(own, got):
    half = own.shape[0] // 2
    return pl.pallas_call(
        halve_kernel,
        out_shape=[
            jax.ShapeDtypeStruct((half, TILE), jnp.float32),
            jax.ShapeDtypeStruct((half, TILE), jnp.bfloat16),
        ],
        in_specs=[vm()] * 2,
        out_specs=[vm()] * 2,
        compiler_params=params(),
        name="halve_sum",
    )(own, got)


def last_kernel(factor, own, got, out):
    out[...] = (own[...] + got[...].astype(jnp.float32)) * factor


def last_sum(factor, own, got):
    return pl.pallas_call(
        functools.partial(last_kernel, factor),
        out_shape=jax.ShapeDtypeStruct(own.shape, jnp.float32),
        in_specs=[vm()] * 2,
        out_specs=vm(),
        compiler_params=params(),
        name="last_sum",
    )(own, got)


def swap(value):
    return lax.ppermute(value, "samp", [(s, s ^ 1) for s in range(16)])


def trade(value, p):
    return lax.ppermute(value, "samp", round_pairs(p))


def after(value, *first):
    return lax.optimization_barrier((value, *first))[0]


def shards(tiles, omega, tile_rows, tile_cols, tile_count):
    kmers = lax.axis_size("kmer")
    other, held, table, lists = forward_first(tile_rows, tile_cols, tile_count, tiles, omega)
    sends = pair_sum(forward_next(NEAR_EARLY, lists, held, table), swap(other))
    held_late = after(held, *sends)
    parts = [trade(s, p) for p, s in enumerate(sends)]
    other = forward_next(FAR_LATE, lists, held_late, table)
    sends = pair_sum(forward_next(NEAR_LATE, lists, held_late, table), swap(other))
    parts += [trade(s, p + 2) for p, s in enumerate(sends)]
    turned = turn(tile_count, after(held, *sends))
    part = part_sum("part_sum", *parts)
    part, turned = lax.optimization_barrier((part, turned))
    chunk = part_sum("chunk_sum", part, swap(part))
    near = [trade(chunk, p) for p in range(4)]
    far = [swap(piece) for piece in near]
    first = backward_early(lists, turned, near[:2], far[:2])
    keep, *shares = backward_late(lists, turned, first, near[2:], far[2:])
    sketch = sketch_rows(after(chunk, *shares))
    got = [lax.ppermute(s, ("kmer", "samp"), y_pairs(r)) for r, s in enumerate(shares)]
    keep, share = line_sum(keep, got)
    keep, share = halve_sum(keep, lax.ppermute(share, "kmer", [(i, i ^ 1) for i in range(16)]))
    got = lax.ppermute(share, "kmer", [(i, i // 4 * 4 + 3 - i % 4) for i in range(16)])
    factor = 1.0 / (KB_DEV * TILE * kmers) ** 0.5
    return sketch, last_sum(factor, keep, got)


def solution(mesh):
    placed = (
        P(("kmer", "samp"), None, None),
        P("samp", None),
        P(("kmer", "samp")),
        P(("kmer", "samp")),
        P(("kmer", "samp")),
    )
    return jax.shard_map(
        shards,
        mesh=mesh,
        in_specs=placed,
        out_specs=(P(("kmer", "samp"), None), P(("samp", "kmer"), None)),
        check_vma=False,
    )
```

```python
import functools

import jax
import jax.numpy as jnp
from jax import lax
from jax.experimental import pallas as pl
from jax.experimental.pallas import tpu as pltpu
from jax.sharding import PartitionSpec as P

TILE = 128
KB_DEV = 56
SB_DEV = 8
CHUNK_BLOCKS = KB_DEV // 8
CHUNK = CHUNK_BLOCKS * TILE
PART_BLOCKS = 2 * CHUNK_BLOCKS
PART = PART_BLOCKS * TILE
UNROLL = 12
LIST = 128
FETCH = 8
VMEM_LIMIT = 48 * 1024 * 1024
COST = pl.CostEstimate(flops=200 * 44 * TILE**3, bytes_accessed=200 * 44 * TILE**2, transcendentals=0)

ROUNDS = (
    ((1, 0), (3, 1)),
    ((3, 0), (1, 1)),
    ((2, 0), (2, 1)),
    ((0, 0), (0, 1)),
)
RELAYS = (((1, 0), (3, 0)), ((3, 0), (1, 0)))
NEAR_EARLY, NEAR_LATE, FAR_EARLY, FAR_LATE = range(4)
LINE = ((2, 2), (1, 3), (3, 1))


def vm():
    return pl.BlockSpec(memory_space=pltpu.VMEM)


def sm():
    return pl.BlockSpec(memory_space=pltpu.SMEM)


def params():
    return pltpu.CompilerParams(vmem_limit_bytes=VMEM_LIMIT)


def place():
    j = lax.axis_index("samp")
    return j // 8, (j // 2) % 4, j % 2


def kmer_place():
    i = lax.axis_index("kmer")
    return i // 4, i % 4


def pairs(moves):
    out = []
    for s in range(16):
        z, x, c = s // 8, (s // 2) % 4, s % 2
        dx, dz = moves[c]
        out.append((s, (z ^ dz) * 8 + (x ^ dx) * 2 + c))
    return out


def y_pairs(r):
    out = []
    for i in range(16):
        for j in range(16):
            to = ((i // 4 + LINE[r][j % 2]) % 4) * 4 + i % 4
            out.append((i * 16 + j, to * 16 + j))
    return out


def block(i):
    return pl.ds(pl.multiple_of(i * TILE, TILE), TILE)


def unpack(word):
    return lax.rem(word, 128), lax.rem(lax.div(word, 128), 64), lax.div(word, 8192)


def size_of(lists, which):
    return lists[which * LIST + LIST - 1]


def list_slots(rows, cols, count, lists, shift, owner):
    cap = rows.shape[0]
    z, x, c = place()
    for m in range(8):
        mx = m % 4
        e = jnp.bitwise_xor(x, mx)
        same_z = (z == m // 4).astype(jnp.int32)
        core = 1 - same_z
        odd = jnp.where(core == 0, e == 3, e == 1).astype(jnp.int32)
        p = jnp.where(e == 0, 3, jnp.where(e == 2, 2, odd))
        late = (p >= 2).astype(jnp.int32)
        shift[m] = (p - 2 * late - m) * CHUNK_BLOCKS
        owner[m] = jnp.where(core == c, 0, 2) + late

    def visit(s, sizes):
        row = rows[s]
        m = (row * 37) >> 8
        word = s + (row + shift[m]) * 128 + cols[s] * 8192
        which = jnp.where(s < count, owner[m], 4)
        for k, n in enumerate(sizes):
            lists[k * LIST + n] = word
        return tuple(n + (which == k).astype(jnp.int32) for k, n in enumerate(sizes))

    sizes = lax.fori_loop(0, cap, visit, (jnp.int32(0),) * 4, unroll=8)
    for k, n in enumerate(sizes):
        pad = lax.rem(lists[k * LIST], 128) + PART_BLOCKS * 128 + SB_DEV * 8192
        for u in range(UNROLL):
            lists[k * LIST + n + u] = pad
        lists[k * LIST + LIST - 1] = n


def forward_slots(lists, which, tiles, omega, acc, out):
    acc[...] = jnp.zeros_like(acc)

    def step(g, carry):
        prods, where = [], []
        for u in range(UNROLL):
            slot, row, col = unpack(lists[which * LIST + g * UNROLL + u])
            col = jnp.minimum(col, SB_DEV - 1)
            where.append(block(row))
            prods.append(
                jnp.dot(tiles[slot], omega[block(col), :], preferred_element_type=jnp.float32)
            )
        for at, prod in zip(where, prods):
            acc[at, :] = acc[at, :] + prod
        return carry

    lax.fori_loop(0, (size_of(lists, which) + UNROLL - 1) // UNROLL, step, 0)
    out[...] = acc[pl.ds(0, PART), :].astype(jnp.bfloat16)


def forward_first_kernel(
    rows, cols, count, tiles, omega, out, held, table, lists, acc, s_rows, s_cols, shift, owner, sems, tile_sems
):
    small = [
        pltpu.make_async_copy(rows, s_rows, sems.at[0]),
        pltpu.make_async_copy(cols, s_cols, sems.at[1]),
    ]
    for copy in small:
        copy.start()
    used = count[0]

    def fetch(g):
        at = pl.ds(g * FETCH, FETCH)
        return pltpu.make_async_copy(tiles.at[at], held.at[at], tile_sems.at[g])

    fetches = tiles.shape[0] // FETCH
    for g in range(fetches):
        pl.when(g * FETCH < used)(fetch(g).start)
    fetch_omega = pltpu.make_async_copy(omega, table, sems.at[2])
    fetch_omega.start()
    for copy in small:
        copy.wait()
    list_slots(s_rows, s_cols, used, lists, shift, owner)
    for g in range(fetches):
        pl.when(g * FETCH < used)(fetch(g).wait)
    fetch_omega.wait()
    forward_slots(lists, FAR_LATE, held, table, acc, out)


def in_hbm(value):
    return pltpu.with_memory_space_constraint(value, pltpu.HBM)


def forward_first(rows, cols, count, tiles, omega):
    cap = tiles.shape[0]
    anywhere = pl.BlockSpec(memory_space=pltpu.HBM)
    return pl.pallas_call(
        forward_first_kernel,
        out_shape=[
            jax.ShapeDtypeStruct((PART, TILE), jnp.bfloat16),
            jax.ShapeDtypeStruct(tiles.shape, tiles.dtype),
            jax.ShapeDtypeStruct(omega.shape, omega.dtype),
            jax.ShapeDtypeStruct((4 * LIST,), jnp.int32),
        ],
        in_specs=[anywhere, anywhere, sm(), anywhere, anywhere],
        out_specs=[vm(), vm(), vm(), sm()],
        scratch_shapes=[
            pltpu.VMEM((PART + TILE, TILE), jnp.float32),
            pltpu.SMEM((cap,), jnp.int32),
            pltpu.SMEM((cap,), jnp.int32),
            pltpu.SMEM((8,), jnp.int32),
            pltpu.SMEM((8,), jnp.int32),
            pltpu.SemaphoreType.DMA((3,)),
            pltpu.SemaphoreType.DMA((cap // FETCH,)),
        ],
        compiler_params=params(),
        name="forward_first",
    )(in_hbm(rows), in_hbm(cols), count, in_hbm(tiles), in_hbm(omega))


def forward_next_kernel(which, lists, held, table, out, acc):
    forward_slots(lists, which, held, table, acc, out)


def forward_next(which, lists, held, table):
    return pl.pallas_call(
        functools.partial(forward_next_kernel, which),
        out_shape=jax.ShapeDtypeStruct((PART, TILE), jnp.bfloat16),
        in_specs=[sm(), vm(), vm()],
        out_specs=vm(),
        scratch_shapes=[pltpu.VMEM((PART + TILE, TILE), jnp.float32)],
        compiler_params=params(),
        cost_estimate=COST,
        name=f"forward_next{which}",
    )(lists, held, table)


def turn_kernel(count, tiles, out):
    def one(g, carry):
        for u in range(4):
            out[g * 4 + u] = tiles[g * 4 + u].T
        return carry

    lax.fori_loop(0, (count[0] + 3) // 4, one, 0)


def turn(count, tiles):
    return pl.pallas_call(
        turn_kernel,
        out_shape=jax.ShapeDtypeStruct(tiles.shape, tiles.dtype),
        in_specs=[sm(), vm()],
        out_specs=vm(),
        compiler_params=params(),
        name="turn_tiles",
    )(count, tiles)


def pair_chunk(a, b, start, rows):
    at = pl.ds(start, rows)
    return a[at, :].astype(jnp.float32) + b[at, :].astype(jnp.float32)


def pair_late_kernel(a, b, low, high, last):
    half = CHUNK // 2
    for q, send in enumerate((low, high)):
        send[...] = pair_chunk(a, b, q * half, half).astype(jnp.bfloat16)
    last[...] = pair_chunk(a, b, CHUNK, CHUNK).astype(jnp.bfloat16)


def pair_late(a, b):
    half = jax.ShapeDtypeStruct((CHUNK // 2, TILE), jnp.bfloat16)
    return pl.pallas_call(
        pair_late_kernel,
        out_shape=[half, half, jax.ShapeDtypeStruct((CHUNK, TILE), jnp.bfloat16)],
        in_specs=[vm(), vm()],
        out_specs=[vm()] * 3,
        compiler_params=params(),
        name="pair_late",
    )(a, b)


def pair_early_kernel(a, b, low, high, s0, s1):
    half = CHUNK // 2
    lower, upper = pl.ds(0, half), pl.ds(half, half)
    s0[lower, :] = pair_chunk(a, b, 0, half).astype(jnp.bfloat16)
    s0[upper, :] = (pair_chunk(a, b, half, half) + high[...].astype(jnp.float32)).astype(jnp.bfloat16)
    s1[lower, :] = (pair_chunk(a, b, CHUNK, half) + low[...].astype(jnp.float32)).astype(jnp.bfloat16)
    s1[upper, :] = pair_chunk(a, b, CHUNK + half, half).astype(jnp.bfloat16)


def pair_early(a, b, low, high):
    shape = jax.ShapeDtypeStruct((CHUNK, TILE), jnp.bfloat16)
    return pl.pallas_call(
        pair_early_kernel,
        out_shape=[shape] * 2,
        in_specs=[vm()] * 4,
        out_specs=[vm()] * 2,
        compiler_params=params(),
        name="pair_early",
    )(a, b, low, high)


def part_kernel(*refs):
    out = refs[-1]
    total = refs[0][...].astype(jnp.float32)
    for ref in refs[1:-1]:
        total = total + ref[...].astype(jnp.float32)
    out[...] = total.astype(jnp.bfloat16)


def part_sum(name, *parts):
    return pl.pallas_call(
        part_kernel,
        out_shape=jax.ShapeDtypeStruct((CHUNK, TILE), jnp.bfloat16),
        in_specs=[vm()] * len(parts),
        out_specs=vm(),
        compiler_params=params(),
        name=name,
    )(*parts)


def backward_slots(lists, which, turned, table, acc):
    def step(g, carry):
        prods, where = [], []
        for u in range(UNROLL):
            slot, row, col = unpack(lists[which * LIST + g * UNROLL + u])
            row = jnp.minimum(row, PART_BLOCKS - 1)
            where.append(block(col))
            prods.append(
                jnp.dot(turned[slot], table[block(row), :], preferred_element_type=jnp.float32)
            )
        for at, prod in zip(where, prods):
            acc[at, :] = acc[at, :] + prod
        return carry

    lax.fori_loop(0, (size_of(lists, which) + UNROLL - 1) // UNROLL, step, 0)


def backward_part(lists, kinds, turned, near, far, table, acc):
    for kind, pieces in zip(kinds, (near, far)):
        start = 0
        for piece in pieces:
            table[pl.ds(start, piece.shape[0]), :] = piece[...]
            start += piece.shape[0]
        backward_slots(lists, kind, turned, table, acc)


def sketch_kernel(chunk, out):
    _, _, c = place()
    size = out.shape[0]
    out[...] = chunk[pl.ds(pl.multiple_of(c * size, size), size), :]


def sketch_rows(chunk):
    return pl.pallas_call(
        sketch_kernel,
        out_shape=jax.ShapeDtypeStruct((CHUNK // 2, TILE), jnp.bfloat16),
        in_specs=[vm()],
        out_specs=vm(),
        compiler_params=params(),
        name="sketch_rows",
    )(chunk)


def backward_early_kernel(lists, turned, n0, n1, f0, f1, out, table):
    out[...] = jnp.zeros_like(out)
    backward_part(lists, (NEAR_EARLY, FAR_EARLY), turned, (n0, n1), (f0, f1), table, out)


def backward_early(lists, turned, near, far):
    return pl.pallas_call(
        backward_early_kernel,
        out_shape=jax.ShapeDtypeStruct(((SB_DEV + 1) * TILE, TILE), jnp.float32),
        in_specs=[sm()] + [vm()] * 5,
        out_specs=vm(),
        scratch_shapes=[pltpu.VMEM((PART, TILE), jnp.bfloat16)],
        compiler_params=params(),
        cost_estimate=COST,
        name="backward_early",
    )(lists, turned, *near, *far)


def line_offset(r):
    _, _, c = place()
    return jnp.where(c == 0, LINE[r][0], LINE[r][1])


def share_at(i, size):
    return pl.ds(pl.multiple_of(lax.rem(i + 4, 4) * size, size), size)


def backward_late_kernel(
    lists, turned, first, nl, nh, n3, fl, fh, f3, keep, s0, s1, s2, acc, table
):
    acc[...] = first[...]
    backward_part(lists, (NEAR_LATE, FAR_LATE), turned, (nl, nh, n3), (fl, fh, f3), table, acc)
    y, _ = kmer_place()
    size = keep.shape[0]
    for r, send in enumerate((s0, s1, s2)):
        send[...] = acc[share_at(y + line_offset(r), size), :].astype(jnp.bfloat16)
    keep[...] = acc[share_at(y, size), :]


def backward_late(lists, turned, first, near, far):
    share = SB_DEV * TILE // 4
    send = jax.ShapeDtypeStruct((share, TILE), jnp.bfloat16)
    return pl.pallas_call(
        backward_late_kernel,
        out_shape=[jax.ShapeDtypeStruct((share, TILE), jnp.float32), send, send, send],
        in_specs=[sm()] + [vm()] * 8,
        out_specs=[vm()] * 4,
        scratch_shapes=[
            pltpu.VMEM(((SB_DEV + 1) * TILE, TILE), jnp.float32),
            pltpu.VMEM((PART, TILE), jnp.bfloat16),
        ],
        compiler_params=params(),
        name="backward_late",
    )(lists, turned, first, *near, *far)


def line_kernel(own, g0, g1, g2, keep, send, acc):
    total = own[...]
    for got in (g0, g1, g2):
        total = total + got[...].astype(jnp.float32)
    acc[...] = total
    _, zh = kmer_place()
    size = keep.shape[0] // 2
    peer = zh + 1 - 2 * lax.rem(zh, 2)
    for k, (mine, theirs) in enumerate(((zh, peer), (3 - zh, 3 - peer))):
        keep[pl.ds(k * size, size), :] = acc[share_at(mine, size), :]
        send[pl.ds(k * size, size), :] = acc[share_at(theirs, size), :].astype(jnp.bfloat16)


def line_sum(own, got):
    half = own.shape[0] // 2
    return pl.pallas_call(
        line_kernel,
        out_shape=[
            jax.ShapeDtypeStruct((half, TILE), jnp.float32),
            jax.ShapeDtypeStruct((half, TILE), jnp.bfloat16),
        ],
        in_specs=[vm()] * 4,
        out_specs=[vm()] * 2,
        scratch_shapes=[pltpu.VMEM(own.shape, jnp.float32)],
        compiler_params=params(),
        name="line_sum",
    )(own, *got)


def halve_kernel(own, got, keep, send):
    size = keep.shape[0]
    total = own[...] + got[...].astype(jnp.float32)
    keep[...] = total[:size]
    send[...] = total[size:].astype(jnp.bfloat16)


def halve_sum(own, got):
    half = own.shape[0] // 2
    return pl.pallas_call(
        halve_kernel,
        out_shape=[
            jax.ShapeDtypeStruct((half, TILE), jnp.float32),
            jax.ShapeDtypeStruct((half, TILE), jnp.bfloat16),
        ],
        in_specs=[vm()] * 2,
        out_specs=[vm()] * 2,
        compiler_params=params(),
        name="halve_sum",
    )(own, got)


def last_kernel(factor, own, got, out):
    out[...] = (own[...] + got[...].astype(jnp.float32)) * factor


def last_sum(factor, own, got):
    return pl.pallas_call(
        functools.partial(last_kernel, factor),
        out_shape=jax.ShapeDtypeStruct(own.shape, jnp.float32),
        in_specs=[vm()] * 2,
        out_specs=vm(),
        compiler_params=params(),
        name="last_sum",
    )(own, got)


def swap(value):
    return lax.ppermute(value, "samp", [(s, s ^ 1) for s in range(16)])


def trade(value, moves):
    return lax.ppermute(value, "samp", pairs(moves))


def after(value, *first):
    return lax.optimization_barrier((value, *first))[0]


def shards(tiles, omega, tile_rows, tile_cols, tile_count):
    kmers = lax.axis_size("kmer")
    other, held, table, lists = forward_first(tile_rows, tile_cols, tile_count, tiles, omega)
    *halves, send3 = pair_late(forward_next(NEAR_LATE, lists, held, table), swap(other))
    held_next = after(held, *halves)
    relayed = [trade(s, m) for s, m in zip(halves, RELAYS)]
    part3 = trade(send3, ROUNDS[3])
    other = forward_next(FAR_EARLY, lists, held_next, table)
    sends = pair_early(forward_next(NEAR_EARLY, lists, held_next, table), swap(other), *relayed)
    parts = [trade(s, m) for s, m in zip(sends, ROUNDS)]
    turned = turn(tile_count, after(held, *sends))
    part = part_sum("part_sum", *parts, part3)
    part, turned = lax.optimization_barrier((part, turned))
    chunk = part_sum("chunk_sum", part, swap(part))
    n0, n1 = trade(chunk, ROUNDS[0]), trade(chunk, ROUNDS[1])
    n3 = trade(chunk, ROUNDS[3])
    high = trade(n0[CHUNK // 2 :], RELAYS[1])
    low = trade(n1[: CHUNK // 2], RELAYS[0])
    first = backward_early(lists, turned, (n0, n1), (swap(n0), swap(n1)))
    near = (low, high, n3)
    far = [swap(piece) for piece in near]
    keep, *shares = backward_late(lists, turned, first, near, far)
    sketch = sketch_rows(after(chunk, *shares))
    got = [lax.ppermute(s, ("kmer", "samp"), y_pairs(r)) for r, s in enumerate(shares)]
    keep, share = line_sum(keep, got)
    keep, share = halve_sum(keep, lax.ppermute(share, "kmer", [(i, i ^ 1) for i in range(16)]))
    got = lax.ppermute(share, "kmer", [(i, i // 4 * 4 + 3 - i % 4) for i in range(16)])
    factor = 1.0 / (KB_DEV * TILE * kmers) ** 0.5
    return sketch, last_sum(factor, keep, got)


def solution(mesh):
    placed = (
        P(("kmer", "samp"), None, None),
        P("samp", None),
        P(("kmer", "samp")),
        P(("kmer", "samp")),
        P(("kmer", "samp")),
    )
    return jax.shard_map(
        shards,
        mesh=mesh,
        in_specs=placed,
        out_specs=(P(("kmer", "samp"), None), P(("samp", "kmer"), None)),
        check_vma=False,
    )
```

```python
import functools

import jax
import jax.numpy as jnp
from jax import lax
from jax.experimental import pallas as pl
from jax.experimental.pallas import tpu as pltpu
from jax.sharding import PartitionSpec as P

TILE = 128
KB_DEV = 56
SB_DEV = 8
CHUNK_BLOCKS = KB_DEV // 8
CHUNK = CHUNK_BLOCKS * TILE
PART_BLOCKS = 2 * CHUNK_BLOCKS
PART = PART_BLOCKS * TILE
UNROLL = 12
LIST = 128
FETCH = 8
VMEM_LIMIT = 48 * 1024 * 1024
COST = pl.CostEstimate(flops=200 * 44 * TILE**3, bytes_accessed=200 * 44 * TILE**2, transcendentals=0)

ROUNDS = (
    ((1, 0), (3, 1)),
    ((3, 0), (1, 1)),
    ((2, 0), (2, 1)),
    ((0, 0), (0, 1)),
)
NEAR_EARLY, NEAR_LATE, FAR_EARLY, FAR_LATE = range(4)
LINE = ((2, 2), (1, 3), (3, 1))


def vm():
    return pl.BlockSpec(memory_space=pltpu.VMEM)


def sm():
    return pl.BlockSpec(memory_space=pltpu.SMEM)


def params():
    return pltpu.CompilerParams(vmem_limit_bytes=VMEM_LIMIT)


def place():
    j = lax.axis_index("samp")
    return j // 8, (j // 2) % 4, j % 2


def kmer_place():
    i = lax.axis_index("kmer")
    return i // 4, i % 4


def round_pairs(p):
    out = []
    for s in range(16):
        z, x, c = s // 8, (s // 2) % 4, s % 2
        dx, dz = ROUNDS[p][c]
        out.append((s, (z ^ dz) * 8 + (x ^ dx) * 2 + c))
    return out


def y_pairs(r):
    out = []
    for i in range(16):
        for j in range(16):
            to = ((i // 4 + LINE[r][j % 2]) % 4) * 4 + i % 4
            out.append((i * 16 + j, to * 16 + j))
    return out


def block(i):
    return pl.ds(pl.multiple_of(i * TILE, TILE), TILE)


def chunk_at(q):
    return pl.ds(q * CHUNK, CHUNK)


def unpack(word):
    return lax.rem(word, 128), lax.rem(lax.div(word, 128), 64), lax.div(word, 8192)


def size_of(lists, which):
    return lists[which * LIST + LIST - 1]


def list_slots(rows, cols, count, lists, shift, owner):
    cap = rows.shape[0]
    z, x, c = place()
    for m in range(8):
        mx = m % 4
        e = jnp.bitwise_xor(x, mx)
        same_z = (z == m // 4).astype(jnp.int32)
        core = 1 - same_z
        odd = jnp.where(core == 0, e == 3, e == 1).astype(jnp.int32)
        p = jnp.where(e == 0, 3, jnp.where(e == 2, 2, odd))
        late = (p >= 2).astype(jnp.int32)
        shift[m] = (p - 2 * late - m) * CHUNK_BLOCKS
        owner[m] = jnp.where(core == c, 0, 2) + late

    def visit(s, sizes):
        row = rows[s]
        m = (row * 37) >> 8
        word = s + (row + shift[m]) * 128 + cols[s] * 8192
        which = jnp.where(s < count, owner[m], 4)
        for k, n in enumerate(sizes):
            lists[k * LIST + n] = word
        return tuple(n + (which == k).astype(jnp.int32) for k, n in enumerate(sizes))

    sizes = lax.fori_loop(0, cap, visit, (jnp.int32(0),) * 4, unroll=8)
    for k, n in enumerate(sizes):
        pad = lax.rem(lists[k * LIST], 128) + PART_BLOCKS * 128 + SB_DEV * 8192
        for u in range(UNROLL):
            lists[k * LIST + n + u] = pad
        lists[k * LIST + LIST - 1] = n


def forward_slots(lists, which, tiles, omega, acc, out):
    acc[...] = jnp.zeros_like(acc)

    def step(g, carry):
        prods, where = [], []
        for u in range(UNROLL):
            slot, row, col = unpack(lists[which * LIST + g * UNROLL + u])
            col = jnp.minimum(col, SB_DEV - 1)
            where.append(block(row))
            prods.append(
                jnp.dot(tiles[slot], omega[block(col), :], preferred_element_type=jnp.float32)
            )
        for at, prod in zip(where, prods):
            acc[at, :] = acc[at, :] + prod
        return carry

    lax.fori_loop(0, (size_of(lists, which) + UNROLL - 1) // UNROLL, step, 0)
    out[...] = acc[pl.ds(0, PART), :].astype(jnp.bfloat16)


def forward_first_kernel(
    rows, cols, count, tiles, omega, out, held, table, lists, acc, s_rows, s_cols, shift, owner, sems, tile_sems
):
    small = [
        pltpu.make_async_copy(rows, s_rows, sems.at[0]),
        pltpu.make_async_copy(cols, s_cols, sems.at[1]),
    ]
    for copy in small:
        copy.start()
    used = count[0]

    def fetch(g):
        at = pl.ds(g * FETCH, FETCH)
        return pltpu.make_async_copy(tiles.at[at], held.at[at], tile_sems.at[g])

    fetches = tiles.shape[0] // FETCH
    for g in range(fetches):
        pl.when(g * FETCH < used)(fetch(g).start)
    fetch_omega = pltpu.make_async_copy(omega, table, sems.at[2])
    fetch_omega.start()
    for copy in small:
        copy.wait()
    list_slots(s_rows, s_cols, used, lists, shift, owner)
    for g in range(fetches):
        pl.when(g * FETCH < used)(fetch(g).wait)
    fetch_omega.wait()
    forward_slots(lists, FAR_LATE, held, table, acc, out)


def in_hbm(value):
    return pltpu.with_memory_space_constraint(value, pltpu.HBM)


def forward_first(rows, cols, count, tiles, omega):
    cap = tiles.shape[0]
    anywhere = pl.BlockSpec(memory_space=pltpu.HBM)
    return pl.pallas_call(
        forward_first_kernel,
        out_shape=[
            jax.ShapeDtypeStruct((PART, TILE), jnp.bfloat16),
            jax.ShapeDtypeStruct(tiles.shape, tiles.dtype),
            jax.ShapeDtypeStruct(omega.shape, omega.dtype),
            jax.ShapeDtypeStruct((4 * LIST,), jnp.int32),
        ],
        in_specs=[anywhere, anywhere, sm(), anywhere, anywhere],
        out_specs=[vm(), vm(), vm(), sm()],
        scratch_shapes=[
            pltpu.VMEM((PART + TILE, TILE), jnp.float32),
            pltpu.SMEM((cap,), jnp.int32),
            pltpu.SMEM((cap,), jnp.int32),
            pltpu.SMEM((8,), jnp.int32),
            pltpu.SMEM((8,), jnp.int32),
            pltpu.SemaphoreType.DMA((3,)),
            pltpu.SemaphoreType.DMA((cap // FETCH,)),
        ],
        compiler_params=params(),
        name="forward_first",
    )(in_hbm(rows), in_hbm(cols), count, in_hbm(tiles), in_hbm(omega))


def forward_next_kernel(which, lists, held, table, out, acc):
    forward_slots(lists, which, held, table, acc, out)


def forward_next(which, lists, held, table):
    return pl.pallas_call(
        functools.partial(forward_next_kernel, which),
        out_shape=jax.ShapeDtypeStruct((PART, TILE), jnp.bfloat16),
        in_specs=[sm(), vm(), vm()],
        out_specs=vm(),
        scratch_shapes=[pltpu.VMEM((PART + TILE, TILE), jnp.float32)],
        compiler_params=params(),
        cost_estimate=COST,
        name=f"forward_next{which}",
    )(lists, held, table)


def turn_kernel(count, tiles, out):
    def one(g, carry):
        for u in range(4):
            out[g * 4 + u] = tiles[g * 4 + u].T
        return carry

    lax.fori_loop(0, (count[0] + 3) // 4, one, 0)


def turn(count, tiles):
    return pl.pallas_call(
        turn_kernel,
        out_shape=jax.ShapeDtypeStruct(tiles.shape, tiles.dtype),
        in_specs=[sm(), vm()],
        out_specs=vm(),
        compiler_params=params(),
        name="turn_tiles",
    )(count, tiles)


def pair_kernel(a, b, *sends):
    for q, send in enumerate(sends):
        at = chunk_at(q)
        send[...] = (a[at, :].astype(jnp.float32) + b[at, :].astype(jnp.float32)).astype(jnp.bfloat16)


def pair_sum(a, b):
    shape = jax.ShapeDtypeStruct((CHUNK, TILE), jnp.bfloat16)
    return pl.pallas_call(
        pair_kernel,
        out_shape=[shape] * 2,
        in_specs=[vm(), vm()],
        out_specs=[vm()] * 2,
        compiler_params=params(),
        name="pair_sum",
    )(a, b)


def part_kernel(*refs):
    out = refs[-1]
    total = refs[0][...].astype(jnp.float32)
    for ref in refs[1:-1]:
        total = total + ref[...].astype(jnp.float32)
    out[...] = total.astype(jnp.bfloat16)


def part_sum(name, *parts):
    return pl.pallas_call(
        part_kernel,
        out_shape=jax.ShapeDtypeStruct((CHUNK, TILE), jnp.bfloat16),
        in_specs=[vm()] * len(parts),
        out_specs=vm(),
        compiler_params=params(),
        name=name,
    )(*parts)


def backward_slots(lists, which, turned, table, acc):
    def step(g, carry):
        prods, where = [], []
        for u in range(UNROLL):
            slot, row, col = unpack(lists[which * LIST + g * UNROLL + u])
            row = jnp.minimum(row, PART_BLOCKS - 1)
            where.append(block(col))
            prods.append(
                jnp.dot(turned[slot], table[block(row), :], preferred_element_type=jnp.float32)
            )
        for at, prod in zip(where, prods):
            acc[at, :] = acc[at, :] + prod
        return carry

    lax.fori_loop(0, (size_of(lists, which) + UNROLL - 1) // UNROLL, step, 0)


def backward_part(lists, kinds, turned, near, far, table, acc):
    for kind, pieces in zip(kinds, (near, far)):
        for q, piece in enumerate(pieces):
            table[chunk_at(q), :] = piece[...]
        backward_slots(lists, kind, turned, table, acc)


def sketch_kernel(chunk, out):
    _, _, c = place()
    size = out.shape[0]
    out[...] = chunk[pl.ds(pl.multiple_of(c * size, size), size), :]


def sketch_rows(chunk):
    return pl.pallas_call(
        sketch_kernel,
        out_shape=jax.ShapeDtypeStruct((CHUNK // 2, TILE), jnp.bfloat16),
        in_specs=[vm()],
        out_specs=vm(),
        compiler_params=params(),
        name="sketch_rows",
    )(chunk)


def backward_early_kernel(lists, turned, n0, n1, f0, f1, out, table):
    out[...] = jnp.zeros_like(out)
    backward_part(lists, (NEAR_EARLY, FAR_EARLY), turned, (n0, n1), (f0, f1), table, out)


def backward_early(lists, turned, near, far):
    return pl.pallas_call(
        backward_early_kernel,
        out_shape=jax.ShapeDtypeStruct(((SB_DEV + 1) * TILE, TILE), jnp.float32),
        in_specs=[sm()] + [vm()] * 5,
        out_specs=vm(),
        scratch_shapes=[pltpu.VMEM((PART, TILE), jnp.bfloat16)],
        compiler_params=params(),
        cost_estimate=COST,
        name="backward_early",
    )(lists, turned, *near, *far)


def line_offset(r):
    _, _, c = place()
    return jnp.where(c == 0, LINE[r][0], LINE[r][1])


def share_at(i, size):
    return pl.ds(pl.multiple_of(lax.rem(i + 4, 4) * size, size), size)


def backward_late_kernel(lists, turned, first, n2, n3, f2, f3, keep, s0, s1, s2, acc, table):
    acc[...] = first[...]
    backward_part(lists, (NEAR_LATE, FAR_LATE), turned, (n2, n3), (f2, f3), table, acc)
    y, _ = kmer_place()
    size = keep.shape[0]
    for r, send in enumerate((s0, s1, s2)):
        send[...] = acc[share_at(y + line_offset(r), size), :].astype(jnp.bfloat16)
    keep[...] = acc[share_at(y, size), :]


def backward_late(lists, turned, first, near, far):
    share = SB_DEV * TILE // 4
    send = jax.ShapeDtypeStruct((share, TILE), jnp.bfloat16)
    return pl.pallas_call(
        backward_late_kernel,
        out_shape=[jax.ShapeDtypeStruct((share, TILE), jnp.float32), send, send, send],
        in_specs=[sm()] + [vm()] * 6,
        out_specs=[vm()] * 4,
        scratch_shapes=[
            pltpu.VMEM(((SB_DEV + 1) * TILE, TILE), jnp.float32),
            pltpu.VMEM((PART, TILE), jnp.bfloat16),
        ],
        compiler_params=params(),
        name="backward_late",
    )(lists, turned, first, *near, *far)


def line_kernel(own, g0, g1, g2, keep, send, acc):
    total = own[...]
    for got in (g0, g1, g2):
        total = total + got[...].astype(jnp.float32)
    acc[...] = total
    _, zh = kmer_place()
    size = keep.shape[0] // 2
    peer = zh + 1 - 2 * lax.rem(zh, 2)
    for k, (mine, theirs) in enumerate(((zh, peer), (3 - zh, 3 - peer))):
        keep[pl.ds(k * size, size), :] = acc[share_at(mine, size), :]
        send[pl.ds(k * size, size), :] = acc[share_at(theirs, size), :].astype(jnp.bfloat16)


def line_sum(own, got):
    half = own.shape[0] // 2
    return pl.pallas_call(
        line_kernel,
        out_shape=[
            jax.ShapeDtypeStruct((half, TILE), jnp.float32),
            jax.ShapeDtypeStruct((half, TILE), jnp.bfloat16),
        ],
        in_specs=[vm()] * 4,
        out_specs=[vm()] * 2,
        scratch_shapes=[pltpu.VMEM(own.shape, jnp.float32)],
        compiler_params=params(),
        name="line_sum",
    )(own, *got)


def halve_kernel(own, got, keep, send):
    size = keep.shape[0]
    total = own[...] + got[...].astype(jnp.float32)
    keep[...] = total[:size]
    send[...] = total[size:].astype(jnp.bfloat16)


def halve_sum(own, got):
    half = own.shape[0] // 2
    return pl.pallas_call(
        halve_kernel,
        out_shape=[
            jax.ShapeDtypeStruct((half, TILE), jnp.float32),
            jax.ShapeDtypeStruct((half, TILE), jnp.bfloat16),
        ],
        in_specs=[vm()] * 2,
        out_specs=[vm()] * 2,
        compiler_params=params(),
        name="halve_sum",
    )(own, got)


def last_kernel(factor, own, got, out):
    out[...] = (own[...] + got[...].astype(jnp.float32)) * factor


def last_sum(factor, own, got):
    return pl.pallas_call(
        functools.partial(last_kernel, factor),
        out_shape=jax.ShapeDtypeStruct(own.shape, jnp.float32),
        in_specs=[vm()] * 2,
        out_specs=vm(),
        compiler_params=params(),
        name="last_sum",
    )(own, got)


def swap(value):
    return lax.ppermute(value, "samp", [(s, s ^ 1) for s in range(16)])


def trade(value, p):
    return lax.ppermute(value, "samp", round_pairs(p))


def after(value, *first):
    return lax.optimization_barrier((value, *first))[0]


def shards(tiles, omega, tile_rows, tile_cols, tile_count):
    kmers = lax.axis_size("kmer")
    other, held, table, lists = forward_first(tile_rows, tile_cols, tile_count, tiles, omega)
    sends = pair_sum(forward_next(NEAR_LATE, lists, held, table), swap(other))
    held_next = after(held, *sends)
    parts = [trade(s, p + 2) for p, s in enumerate(sends)]
    other = forward_next(FAR_EARLY, lists, held_next, table)
    sends = pair_sum(forward_next(NEAR_EARLY, lists, held_next, table), swap(other))
    parts += [trade(s, p) for p, s in enumerate(sends)]
    turned = turn(tile_count, after(held, *sends))
    part = part_sum("part_sum", *parts)
    part, turned = lax.optimization_barrier((part, turned))
    chunk = part_sum("chunk_sum", part, swap(part))
    near = [trade(chunk, p) for p in range(4)]
    far = [swap(piece) for piece in near]
    first = backward_early(lists, turned, near[:2], far[:2])
    keep, *shares = backward_late(lists, turned, first, near[2:], far[2:])
    sketch = sketch_rows(after(chunk, *shares))
    got = [lax.ppermute(s, ("kmer", "samp"), y_pairs(r)) for r, s in enumerate(shares)]
    keep, share = line_sum(keep, got)
    keep, share = halve_sum(keep, lax.ppermute(share, "kmer", [(i, i ^ 1) for i in range(16)]))
    got = lax.ppermute(share, "kmer", [(i, i // 4 * 4 + 3 - i % 4) for i in range(16)])
    factor = 1.0 / (KB_DEV * TILE * kmers) ** 0.5
    return sketch, last_sum(factor, keep, got)


def solution(mesh):
    placed = (
        P(("kmer", "samp"), None, None),
        P("samp", None),
        P(("kmer", "samp")),
        P(("kmer", "samp")),
        P(("kmer", "samp")),
    )
    return jax.shard_map(
        shards,
        mesh=mesh,
        in_specs=placed,
        out_specs=(P(("kmer", "samp"), None), P(("samp", "kmer"), None)),
        check_vma=False,
    )
```

```python
import functools

import jax
import jax.numpy as jnp
from jax import lax
from jax.experimental import pallas as pl
from jax.experimental.pallas import tpu as pltpu
from jax.sharding import PartitionSpec as P

TILE = 128
KB_DEV = 56
SB_DEV = 8
CHUNK_BLOCKS = KB_DEV // 8
CHUNK = CHUNK_BLOCKS * TILE
PART_BLOCKS = 2 * CHUNK_BLOCKS
PART = PART_BLOCKS * TILE
UNROLL = 12
PIECE = 448
LIST = 128
FETCH = 8
VMEM_LIMIT = 48 * 1024 * 1024
COST = pl.CostEstimate(flops=200 * 44 * TILE**3, bytes_accessed=200 * 44 * TILE**2, transcendentals=0)

ROUNDS = (
    ((1, 0), (3, 1)),
    ((3, 0), (1, 1)),
    ((2, 0), (2, 1)),
    ((0, 0), (0, 1)),
)
NEAR_EARLY, NEAR_LATE, FAR_EARLY, FAR_LATE = range(4)
LINE = ((2, 2), (1, 3), (3, 1))


def vm():
    return pl.BlockSpec(memory_space=pltpu.VMEM)


def sm():
    return pl.BlockSpec(memory_space=pltpu.SMEM)


def params():
    return pltpu.CompilerParams(vmem_limit_bytes=VMEM_LIMIT)


def place():
    j = lax.axis_index("samp")
    return j // 8, (j // 2) % 4, j % 2


def kmer_place():
    i = lax.axis_index("kmer")
    return i // 4, i % 4


def round_pairs(p):
    out = []
    for s in range(16):
        z, x, c = s // 8, (s // 2) % 4, s % 2
        dx, dz = ROUNDS[p][c]
        out.append((s, (z ^ dz) * 8 + (x ^ dx) * 2 + c))
    return out


def y_pairs(r):
    out = []
    for i in range(16):
        for j in range(16):
            to = ((i // 4 + LINE[r][j % 2]) % 4) * 4 + i % 4
            out.append((i * 16 + j, to * 16 + j))
    return out


def block(i):
    return pl.ds(pl.multiple_of(i * TILE, TILE), TILE)


def chunk_at(q):
    return pl.ds(q * CHUNK, CHUNK)


def unpack(word):
    return lax.rem(word, 128), lax.rem(lax.div(word, 128), 64), lax.div(word, 8192)


def size_of(lists, which):
    return lists[which * LIST + LIST - 1]


def list_slots(rows, cols, count, lists, shift, owner):
    cap = rows.shape[0]
    z, x, c = place()
    for m in range(8):
        mx = m % 4
        e = jnp.bitwise_xor(x, mx)
        same_z = (z == m // 4).astype(jnp.int32)
        core = 1 - same_z
        odd = jnp.where(core == 0, e == 3, e == 1).astype(jnp.int32)
        p = jnp.where(e == 0, 3, jnp.where(e == 2, 2, odd))
        late = (p >= 2).astype(jnp.int32)
        shift[m] = (p - 2 * late - m) * CHUNK_BLOCKS
        owner[m] = jnp.where(core == c, 0, 2) + late

    def visit(s, sizes):
        row = rows[s]
        m = (row * 37) >> 8
        word = s + (row + shift[m]) * 128 + cols[s] * 8192
        which = jnp.where(s < count, owner[m], 4)
        for k, n in enumerate(sizes):
            lists[k * LIST + n] = word
        return tuple(n + (which == k).astype(jnp.int32) for k, n in enumerate(sizes))

    sizes = lax.fori_loop(0, cap, visit, (jnp.int32(0),) * 4, unroll=8)
    for k, n in enumerate(sizes):
        pad = lax.rem(lists[k * LIST], 128) + PART_BLOCKS * 128 + SB_DEV * 8192
        for u in range(UNROLL):
            lists[k * LIST + n + u] = pad
        lists[k * LIST + LIST - 1] = n


def forward_slots(lists, which, tiles, omega, acc, out):
    acc[...] = jnp.zeros_like(acc)

    def step(g, carry):
        prods, where = [], []
        for u in range(UNROLL):
            slot, row, col = unpack(lists[which * LIST + g * UNROLL + u])
            col = jnp.minimum(col, SB_DEV - 1)
            where.append(block(row))
            prods.append(
                jnp.dot(tiles[slot], omega[block(col), :], preferred_element_type=jnp.float32)
            )
        for at, prod in zip(where, prods):
            acc[at, :] = acc[at, :] + prod
        return carry

    lax.fori_loop(0, (size_of(lists, which) + UNROLL - 1) // UNROLL, step, 0)
    out[...] = acc[pl.ds(0, PART), :].astype(jnp.bfloat16)


def forward_first_kernel(
    rows, cols, count, tiles, omega, out, held, table, lists, acc, s_rows, s_cols, shift, owner, sems, tile_sems
):
    small = [
        pltpu.make_async_copy(rows, s_rows, sems.at[0]),
        pltpu.make_async_copy(cols, s_cols, sems.at[1]),
    ]
    for copy in small:
        copy.start()
    used = count[0]

    def fetch(g):
        at = pl.ds(g * FETCH, FETCH)
        return pltpu.make_async_copy(tiles.at[at], held.at[at], tile_sems.at[g])

    fetches = tiles.shape[0] // FETCH
    for g in range(fetches):
        pl.when(g * FETCH < used)(fetch(g).start)
    fetch_omega = pltpu.make_async_copy(omega, table, sems.at[2])
    fetch_omega.start()
    for copy in small:
        copy.wait()
    list_slots(s_rows, s_cols, used, lists, shift, owner)
    for g in range(fetches):
        pl.when(g * FETCH < used)(fetch(g).wait)
    fetch_omega.wait()
    forward_slots(lists, FAR_EARLY, held, table, acc, out)


def in_hbm(value):
    return pltpu.with_memory_space_constraint(value, pltpu.HBM)


def forward_first(rows, cols, count, tiles, omega):
    cap = tiles.shape[0]
    anywhere = pl.BlockSpec(memory_space=pltpu.HBM)
    return pl.pallas_call(
        forward_first_kernel,
        out_shape=[
            jax.ShapeDtypeStruct((PART, TILE), jnp.bfloat16),
            jax.ShapeDtypeStruct(tiles.shape, tiles.dtype),
            jax.ShapeDtypeStruct(omega.shape, omega.dtype),
            jax.ShapeDtypeStruct((4 * LIST,), jnp.int32),
        ],
        in_specs=[anywhere, anywhere, sm(), anywhere, anywhere],
        out_specs=[vm(), vm(), vm(), sm()],
        scratch_shapes=[
            pltpu.VMEM((PART + TILE, TILE), jnp.float32),
            pltpu.SMEM((cap,), jnp.int32),
            pltpu.SMEM((cap,), jnp.int32),
            pltpu.SMEM((8,), jnp.int32),
            pltpu.SMEM((8,), jnp.int32),
            pltpu.SemaphoreType.DMA((3,)),
            pltpu.SemaphoreType.DMA((cap // FETCH,)),
        ],
        compiler_params=params(),
        name="forward_first",
    )(in_hbm(rows), in_hbm(cols), count, in_hbm(tiles), in_hbm(omega))


def forward_next_kernel(which, lists, held, table, out, acc):
    forward_slots(lists, which, held, table, acc, out)


def forward_next(which, lists, held, table):
    return pl.pallas_call(
        functools.partial(forward_next_kernel, which),
        out_shape=jax.ShapeDtypeStruct((PART, TILE), jnp.bfloat16),
        in_specs=[sm(), vm(), vm()],
        out_specs=vm(),
        scratch_shapes=[pltpu.VMEM((PART + TILE, TILE), jnp.float32)],
        compiler_params=params(),
        cost_estimate=COST,
        name=f"forward_next{which}",
    )(lists, held, table)


def turn_kernel(count, tiles, out):
    def one(g, carry):
        for u in range(4):
            out[g * 4 + u] = tiles[g * 4 + u].T
        return carry

    lax.fori_loop(0, (count[0] + 3) // 4, one, 0)


def turn(count, tiles):
    return pl.pallas_call(
        turn_kernel,
        out_shape=jax.ShapeDtypeStruct(tiles.shape, tiles.dtype),
        in_specs=[sm(), vm()],
        out_specs=vm(),
        compiler_params=params(),
        name="turn_tiles",
    )(count, tiles)


def pair_kernel(a, b, *sends):
    for q, send in enumerate(sends):
        at = chunk_at(q)
        send[...] = (a[at, :].astype(jnp.float32) + b[at, :].astype(jnp.float32)).astype(jnp.bfloat16)


def pair_sum(a, b):
    shape = jax.ShapeDtypeStruct((CHUNK, TILE), jnp.bfloat16)
    return pl.pallas_call(
        pair_kernel,
        out_shape=[shape] * 2,
        in_specs=[vm(), vm()],
        out_specs=[vm()] * 2,
        compiler_params=params(),
        name="pair_sum",
    )(a, b)


def part_kernel(*refs):
    out = refs[-1]
    total = refs[0][...].astype(jnp.float32)
    for ref in refs[1:-1]:
        total = total + ref[...].astype(jnp.float32)
    out[...] = total.astype(jnp.bfloat16)


def part_sum(name, *parts):
    return pl.pallas_call(
        part_kernel,
        out_shape=jax.ShapeDtypeStruct((CHUNK, TILE), jnp.bfloat16),
        in_specs=[vm()] * len(parts),
        out_specs=vm(),
        compiler_params=params(),
        name=name,
    )(*parts)


def backward_slots(lists, which, turned, table, acc):
    def step(g, carry):
        prods, where = [], []
        for u in range(UNROLL):
            slot, row, col = unpack(lists[which * LIST + g * UNROLL + u])
            row = jnp.minimum(row, PART_BLOCKS - 1)
            where.append(block(col))
            prods.append(
                jnp.dot(turned[slot], table[block(row), :], preferred_element_type=jnp.float32)
            )
        for at, prod in zip(where, prods):
            acc[at, :] = acc[at, :] + prod
        return carry

    lax.fori_loop(0, (size_of(lists, which) + UNROLL - 1) // UNROLL, step, 0)


def sketch_kernel(chunk, out):
    _, _, c = place()
    size = out.shape[0]
    out[...] = chunk[pl.ds(pl.multiple_of(c * size, size), size), :]


def sketch_rows(chunk):
    return pl.pallas_call(
        sketch_kernel,
        out_shape=jax.ShapeDtypeStruct((CHUNK // 2, TILE), jnp.bfloat16),
        in_specs=[vm()],
        out_specs=vm(),
        compiler_params=params(),
        name="sketch_rows",
    )(chunk)


def backward_part(lists, which, pieces, turned, table, acc):
    start = 0
    for piece in pieces:
        table[pl.ds(start, piece.shape[0]), :] = piece[...]
        start += piece.shape[0]
    backward_slots(lists, which, turned, table, acc)


def backward_early_kernel(lists, turned, n0, n1, *refs):
    *far, out, table = refs
    out[...] = jnp.zeros_like(out)
    backward_part(lists, NEAR_EARLY, (n0, n1), turned, table, out)
    backward_part(lists, FAR_EARLY, far, turned, table, out)


def backward_early(lists, turned, near, far):
    return pl.pallas_call(
        backward_early_kernel,
        out_shape=jax.ShapeDtypeStruct(((SB_DEV + 1) * TILE, TILE), jnp.float32),
        in_specs=[sm()] + [vm()] * (3 + len(far)),
        out_specs=vm(),
        scratch_shapes=[pltpu.VMEM((PART, TILE), jnp.bfloat16)],
        compiler_params=params(),
        cost_estimate=pl.CostEstimate(flops=1, bytes_accessed=1, transcendentals=0),
        name="backward_early",
    )(lists, turned, *near, *far)


def line_offset(r):
    _, _, c = place()
    return jnp.where(c == 0, LINE[r][0], LINE[r][1])


def share_at(i, size):
    return pl.ds(pl.multiple_of(lax.rem(i + 4, 4) * size, size), size)


def backward_late_kernel(
    lists, turned, first, n2, n3, f2, f3, keep, s0, s1, s2, acc, table
):
    acc[...] = first[...]
    backward_part(lists, NEAR_LATE, (n2, n3), turned, table, acc)
    backward_part(lists, FAR_LATE, (f2, f3), turned, table, acc)
    y, _ = kmer_place()
    size = keep.shape[0]
    for r, send in enumerate((s0, s1, s2)):
        send[...] = acc[share_at(y + line_offset(r), size), :].astype(jnp.bfloat16)
    keep[...] = acc[share_at(y, size), :]


def backward_late(lists, turned, first, *pieces):
    share = SB_DEV * TILE // 4
    send = jax.ShapeDtypeStruct((share, TILE), jnp.bfloat16)
    return pl.pallas_call(
        backward_late_kernel,
        out_shape=[jax.ShapeDtypeStruct((share, TILE), jnp.float32), send, send, send],
        in_specs=[sm()] + [vm()] * 6,
        out_specs=[vm()] * 4,
        scratch_shapes=[
            pltpu.VMEM(((SB_DEV + 1) * TILE, TILE), jnp.float32),
            pltpu.VMEM((PART, TILE), jnp.bfloat16),
        ],
        compiler_params=params(),
        name="backward_late",
    )(lists, turned, first, *pieces)


def line_kernel(own, g0, g1, g2, keep, send, acc):
    total = own[...]
    for got in (g0, g1, g2):
        total = total + got[...].astype(jnp.float32)
    acc[...] = total
    _, zh = kmer_place()
    size = keep.shape[0] // 2
    peer = zh + 1 - 2 * lax.rem(zh, 2)
    for k, (mine, theirs) in enumerate(((zh, peer), (3 - zh, 3 - peer))):
        keep[pl.ds(k * size, size), :] = acc[share_at(mine, size), :]
        send[pl.ds(k * size, size), :] = acc[share_at(theirs, size), :].astype(jnp.bfloat16)


def line_sum(own, got):
    half = own.shape[0] // 2
    return pl.pallas_call(
        line_kernel,
        out_shape=[
            jax.ShapeDtypeStruct((half, TILE), jnp.float32),
            jax.ShapeDtypeStruct((half, TILE), jnp.bfloat16),
        ],
        in_specs=[vm()] * 4,
        out_specs=[vm()] * 2,
        scratch_shapes=[pltpu.VMEM(own.shape, jnp.float32)],
        compiler_params=params(),
        name="line_sum",
    )(own, *got)


def halve_kernel(own, got, keep, send):
    size = keep.shape[0]
    total = own[...] + got[...].astype(jnp.float32)
    keep[...] = total[:size]
    send[...] = total[size:].astype(jnp.bfloat16)


def halve_sum(own, got):
    half = own.shape[0] // 2
    return pl.pallas_call(
        halve_kernel,
        out_shape=[
            jax.ShapeDtypeStruct((half, TILE), jnp.float32),
            jax.ShapeDtypeStruct((half, TILE), jnp.bfloat16),
        ],
        in_specs=[vm()] * 2,
        out_specs=[vm()] * 2,
        compiler_params=params(),
        name="halve_sum",
    )(own, got)


def last_kernel(factor, own, got, out):
    out[...] = (own[...] + got[...].astype(jnp.float32)) * factor


def last_sum(factor, own, got):
    return pl.pallas_call(
        functools.partial(last_kernel, factor),
        out_shape=jax.ShapeDtypeStruct(own.shape, jnp.float32),
        in_specs=[vm()] * 2,
        out_specs=vm(),
        compiler_params=params(),
        name="last_sum",
    )(own, got)


def swap(value):
    return lax.ppermute(value, "samp", [(s, s ^ 1) for s in range(16)])


def trade(value, p):
    return lax.ppermute(value, "samp", round_pairs(p))


def after(value, *first):
    return lax.optimization_barrier((value, *first))[0]


def shards(tiles, omega, tile_rows, tile_cols, tile_count):
    kmers = lax.axis_size("kmer")
    other, held, table, lists = forward_first(tile_rows, tile_cols, tile_count, tiles, omega)
    sends = pair_sum(forward_next(NEAR_EARLY, lists, held, table), swap(other))
    held_late = after(held, *sends)
    parts = [trade(s, p) for p, s in enumerate(sends)]
    other = forward_next(FAR_LATE, lists, held_late, table)
    sends = pair_sum(forward_next(NEAR_LATE, lists, held_late, table), swap(other))
    parts += [trade(s, p + 2) for p, s in enumerate(sends)]
    turned = turn(tile_count, after(held, *sends))
    part = part_sum("part_sum", *parts)
    part, turned = lax.optimization_barrier((part, turned))
    chunk = part_sum("chunk_sum", part, swap(part))
    near = [trade(chunk, p) for p in range(4)]
    far = [swap(piece[r : r + PIECE]) for piece in near[:2] for r in range(0, CHUNK, PIECE)]
    first = backward_early(lists, turned, near[:2], far)
    *late, first = lax.optimization_barrier((*near[2:], first))
    keep, *shares = backward_late(lists, turned, first, *late, *(swap(piece) for piece in late))
    sketch = sketch_rows(after(chunk, *shares))
    got = [lax.ppermute(s, ("kmer", "samp"), y_pairs(r)) for r, s in enumerate(shares)]
    keep, share = line_sum(keep, got)
    keep, share = halve_sum(keep, lax.ppermute(share, "kmer", [(i, i ^ 1) for i in range(16)]))
    got = lax.ppermute(share, "kmer", [(i, i // 4 * 4 + 3 - i % 4) for i in range(16)])
    factor = 1.0 / (KB_DEV * TILE * kmers) ** 0.5
    return sketch, last_sum(factor, keep, got)


def solution(mesh):
    placed = (
        P(("kmer", "samp"), None, None),
        P("samp", None),
        P(("kmer", "samp")),
        P(("kmer", "samp")),
        P(("kmer", "samp")),
    )
    return jax.shard_map(
        shards,
        mesh=mesh,
        in_specs=placed,
        out_specs=(P(("kmer", "samp"), None), P(("samp", "kmer"), None)),
        check_vma=False,
    )
```

```python
import functools

import jax
import jax.numpy as jnp
from jax import lax
from jax.experimental import pallas as pl
from jax.experimental.pallas import tpu as pltpu
from jax.sharding import PartitionSpec as P

TILE = 128
KB_DEV = 56
SB_DEV = 8
CHUNK_BLOCKS = KB_DEV // 8
CHUNK = CHUNK_BLOCKS * TILE
PART_BLOCKS = 2 * CHUNK_BLOCKS
PART = PART_BLOCKS * TILE
UNROLL = 12
LIST = 128
FETCH = 8
VMEM_LIMIT = 48 * 1024 * 1024
COST = pl.CostEstimate(flops=200 * 44 * TILE**3, bytes_accessed=200 * 44 * TILE**2, transcendentals=0)

ROUNDS = (
    ((1, 0), (3, 1)),
    ((2, 0), (2, 1)),
    ((3, 0), (1, 1)),
    ((0, 0), (0, 1)),
)
NEAR_EARLY, NEAR_LATE, FAR_EARLY, FAR_LATE = range(4)
LINE = ((2, 2), (1, 3), (3, 1))


def vm():
    return pl.BlockSpec(memory_space=pltpu.VMEM)


def sm():
    return pl.BlockSpec(memory_space=pltpu.SMEM)


def params():
    return pltpu.CompilerParams(vmem_limit_bytes=VMEM_LIMIT)


def place():
    j = lax.axis_index("samp")
    return j // 8, (j // 2) % 4, j % 2


def kmer_place():
    i = lax.axis_index("kmer")
    return i // 4, i % 4


def round_pairs(p):
    out = []
    for s in range(16):
        z, x, c = s // 8, (s // 2) % 4, s % 2
        dx, dz = ROUNDS[p][c]
        out.append((s, (z ^ dz) * 8 + (x ^ dx) * 2 + c))
    return out


def y_pairs(r):
    out = []
    for i in range(16):
        for j in range(16):
            to = ((i // 4 + LINE[r][j % 2]) % 4) * 4 + i % 4
            out.append((i * 16 + j, to * 16 + j))
    return out


def block(i):
    return pl.ds(pl.multiple_of(i * TILE, TILE), TILE)


def chunk_at(q):
    return pl.ds(q * CHUNK, CHUNK)


def unpack(word):
    return lax.rem(word, 128), lax.rem(lax.div(word, 128), 64), lax.div(word, 8192)


def size_of(lists, which):
    return lists[which * LIST + LIST - 1]


def list_slots(rows, cols, count, lists, shift, owner):
    cap = rows.shape[0]
    z, x, c = place()
    for m in range(8):
        mx = m % 4
        e = jnp.bitwise_xor(x, mx)
        same_z = (z == m // 4).astype(jnp.int32)
        core = 1 - same_z
        odd = jnp.where(core == 0, e == 3, e == 1).astype(jnp.int32)
        p = jnp.where(e == 0, 3, jnp.where(e == 2, 1, 2 * odd))
        late = (p >= 2).astype(jnp.int32)
        shift[m] = (p - 2 * late - m) * CHUNK_BLOCKS
        owner[m] = jnp.where(core == c, 0, 2) + late

    def visit(s, sizes):
        row = rows[s]
        m = (row * 37) >> 8
        word = s + (row + shift[m]) * 128 + cols[s] * 8192
        which = jnp.where(s < count, owner[m], 4)
        for k, n in enumerate(sizes):
            lists[k * LIST + n] = word
        return tuple(n + (which == k).astype(jnp.int32) for k, n in enumerate(sizes))

    sizes = lax.fori_loop(0, cap, visit, (jnp.int32(0),) * 4, unroll=8)
    for k, n in enumerate(sizes):
        pad = lax.rem(lists[k * LIST], 128) + PART_BLOCKS * 128 + SB_DEV * 8192
        for u in range(UNROLL):
            lists[k * LIST + n + u] = pad
        lists[k * LIST + LIST - 1] = n


def forward_slots(lists, which, tiles, omega, acc, out):
    acc[...] = jnp.zeros_like(acc)

    def step(g, carry):
        prods, where = [], []
        for u in range(UNROLL):
            slot, row, col = unpack(lists[which * LIST + g * UNROLL + u])
            col = jnp.minimum(col, SB_DEV - 1)
            where.append(block(row))
            prods.append(
                jnp.dot(tiles[slot], omega[block(col), :], preferred_element_type=jnp.float32)
            )
        for at, prod in zip(where, prods):
            acc[at, :] = acc[at, :] + prod
        return carry

    lax.fori_loop(0, (size_of(lists, which) + UNROLL - 1) // UNROLL, step, 0)
    out[...] = acc[pl.ds(0, PART), :].astype(jnp.bfloat16)


def forward_first_kernel(
    rows, cols, count, tiles, omega, out, held, table, lists, acc, s_rows, s_cols, shift, owner, sems, tile_sems
):
    small = [
        pltpu.make_async_copy(rows, s_rows, sems.at[0]),
        pltpu.make_async_copy(cols, s_cols, sems.at[1]),
    ]
    for copy in small:
        copy.start()
    used = count[0]

    def fetch(g):
        at = pl.ds(g * FETCH, FETCH)
        return pltpu.make_async_copy(tiles.at[at], held.at[at], tile_sems.at[g])

    fetches = tiles.shape[0] // FETCH
    for g in range(fetches):
        pl.when(g * FETCH < used)(fetch(g).start)
    fetch_omega = pltpu.make_async_copy(omega, table, sems.at[2])
    fetch_omega.start()
    for copy in small:
        copy.wait()
    list_slots(s_rows, s_cols, used, lists, shift, owner)
    for g in range(fetches):
        pl.when(g * FETCH < used)(fetch(g).wait)
    fetch_omega.wait()
    forward_slots(lists, FAR_EARLY, held, table, acc, out)


def in_hbm(value):
    return pltpu.with_memory_space_constraint(value, pltpu.HBM)


def forward_first(rows, cols, count, tiles, omega):
    cap = tiles.shape[0]
    anywhere = pl.BlockSpec(memory_space=pltpu.HBM)
    return pl.pallas_call(
        forward_first_kernel,
        out_shape=[
            jax.ShapeDtypeStruct((PART, TILE), jnp.bfloat16),
            jax.ShapeDtypeStruct(tiles.shape, tiles.dtype),
            jax.ShapeDtypeStruct(omega.shape, omega.dtype),
            jax.ShapeDtypeStruct((4 * LIST,), jnp.int32),
        ],
        in_specs=[anywhere, anywhere, sm(), anywhere, anywhere],
        out_specs=[vm(), vm(), vm(), sm()],
        scratch_shapes=[
            pltpu.VMEM((PART + TILE, TILE), jnp.float32),
            pltpu.SMEM((cap,), jnp.int32),
            pltpu.SMEM((cap,), jnp.int32),
            pltpu.SMEM((8,), jnp.int32),
            pltpu.SMEM((8,), jnp.int32),
            pltpu.SemaphoreType.DMA((3,)),
            pltpu.SemaphoreType.DMA((cap // FETCH,)),
        ],
        compiler_params=params(),
        name="forward_first",
    )(in_hbm(rows), in_hbm(cols), count, in_hbm(tiles), in_hbm(omega))


def forward_next_kernel(which, lists, held, table, out, acc):
    forward_slots(lists, which, held, table, acc, out)


def forward_next(which, lists, held, table):
    return pl.pallas_call(
        functools.partial(forward_next_kernel, which),
        out_shape=jax.ShapeDtypeStruct((PART, TILE), jnp.bfloat16),
        in_specs=[sm(), vm(), vm()],
        out_specs=vm(),
        scratch_shapes=[pltpu.VMEM((PART + TILE, TILE), jnp.float32)],
        compiler_params=params(),
        cost_estimate=COST,
        name=f"forward_next{which}",
    )(lists, held, table)


def turn_kernel(count, tiles, out):
    def one(g, carry):
        for u in range(4):
            out[g * 4 + u] = tiles[g * 4 + u].T
        return carry

    lax.fori_loop(0, (count[0] + 3) // 4, one, 0)


def turn(count, tiles):
    return pl.pallas_call(
        turn_kernel,
        out_shape=jax.ShapeDtypeStruct(tiles.shape, tiles.dtype),
        in_specs=[sm(), vm()],
        out_specs=vm(),
        compiler_params=params(),
        name="turn_tiles",
    )(count, tiles)


def pair_kernel(a, b, *sends):
    for q, send in enumerate(sends):
        at = chunk_at(q)
        send[...] = (a[at, :].astype(jnp.float32) + b[at, :].astype(jnp.float32)).astype(jnp.bfloat16)


def pair_sum(a, b):
    shape = jax.ShapeDtypeStruct((CHUNK, TILE), jnp.bfloat16)
    return pl.pallas_call(
        pair_kernel,
        out_shape=[shape] * 2,
        in_specs=[vm(), vm()],
        out_specs=[vm()] * 2,
        compiler_params=params(),
        name="pair_sum",
    )(a, b)


def part_kernel(*refs):
    out = refs[-1]
    total = refs[0][...].astype(jnp.float32)
    for ref in refs[1:-1]:
        total = total + ref[...].astype(jnp.float32)
    out[...] = total.astype(jnp.bfloat16)


def part_sum(name, *parts):
    return pl.pallas_call(
        part_kernel,
        out_shape=jax.ShapeDtypeStruct((CHUNK, TILE), jnp.bfloat16),
        in_specs=[vm()] * len(parts),
        out_specs=vm(),
        compiler_params=params(),
        name=name,
    )(*parts)


def backward_slots(lists, which, turned, table, acc):
    def step(g, carry):
        prods, where = [], []
        for u in range(UNROLL):
            slot, row, col = unpack(lists[which * LIST + g * UNROLL + u])
            row = jnp.minimum(row, PART_BLOCKS - 1)
            where.append(block(col))
            prods.append(
                jnp.dot(turned[slot], table[block(row), :], preferred_element_type=jnp.float32)
            )
        for at, prod in zip(where, prods):
            acc[at, :] = acc[at, :] + prod
        return carry

    lax.fori_loop(0, (size_of(lists, which) + UNROLL - 1) // UNROLL, step, 0)


def backward_part(lists, kinds, turned, near, far, table, acc):
    for kind, pieces in zip(kinds, (near, far)):
        for q, piece in enumerate(pieces):
            table[chunk_at(q), :] = piece[...]
        backward_slots(lists, kind, turned, table, acc)


def sketch_kernel(chunk, out):
    _, _, c = place()
    size = out.shape[0]
    out[...] = chunk[pl.ds(pl.multiple_of(c * size, size), size), :]


def sketch_rows(chunk):
    return pl.pallas_call(
        sketch_kernel,
        out_shape=jax.ShapeDtypeStruct((CHUNK // 2, TILE), jnp.bfloat16),
        in_specs=[vm()],
        out_specs=vm(),
        compiler_params=params(),
        name="sketch_rows",
    )(chunk)


def backward_early_kernel(lists, turned, n0, n1, f0, f1, out, table):
    out[...] = jnp.zeros_like(out)
    backward_part(lists, (NEAR_EARLY, FAR_EARLY), turned, (n0, n1), (f0, f1), table, out)


def backward_early(lists, turned, near, far):
    return pl.pallas_call(
        backward_early_kernel,
        out_shape=jax.ShapeDtypeStruct(((SB_DEV + 1) * TILE, TILE), jnp.float32),
        in_specs=[sm()] + [vm()] * 5,
        out_specs=vm(),
        scratch_shapes=[pltpu.VMEM((PART, TILE), jnp.bfloat16)],
        compiler_params=params(),
        cost_estimate=COST,
        name="backward_early",
    )(lists, turned, *near, *far)


def line_offset(r):
    _, _, c = place()
    return jnp.where(c == 0, LINE[r][0], LINE[r][1])


def share_at(i, size):
    return pl.ds(pl.multiple_of(lax.rem(i + 4, 4) * size, size), size)


def backward_late_kernel(lists, turned, first, n2, n3, f2, f3, keep, s0, s1, s2, acc, table):
    acc[...] = first[...]
    backward_part(lists, (NEAR_LATE, FAR_LATE), turned, (n2, n3), (f2, f3), table, acc)
    y, _ = kmer_place()
    size = keep.shape[0]
    for r, send in enumerate((s0, s1, s2)):
        send[...] = acc[share_at(y + line_offset(r), size), :].astype(jnp.bfloat16)
    keep[...] = acc[share_at(y, size), :]


def backward_late(lists, turned, first, near, far):
    share = SB_DEV * TILE // 4
    send = jax.ShapeDtypeStruct((share, TILE), jnp.bfloat16)
    return pl.pallas_call(
        backward_late_kernel,
        out_shape=[jax.ShapeDtypeStruct((share, TILE), jnp.float32), send, send, send],
        in_specs=[sm()] + [vm()] * 6,
        out_specs=[vm()] * 4,
        scratch_shapes=[
            pltpu.VMEM(((SB_DEV + 1) * TILE, TILE), jnp.float32),
            pltpu.VMEM((PART, TILE), jnp.bfloat16),
        ],
        compiler_params=params(),
        name="backward_late",
    )(lists, turned, first, *near, *far)


def line_kernel(own, g0, g1, g2, keep, send, acc):
    total = own[...]
    for got in (g0, g1, g2):
        total = total + got[...].astype(jnp.float32)
    acc[...] = total
    _, zh = kmer_place()
    size = keep.shape[0] // 2
    peer = zh + 1 - 2 * lax.rem(zh, 2)
    for k, (mine, theirs) in enumerate(((zh, peer), (3 - zh, 3 - peer))):
        keep[pl.ds(k * size, size), :] = acc[share_at(mine, size), :]
        send[pl.ds(k * size, size), :] = acc[share_at(theirs, size), :].astype(jnp.bfloat16)


def line_sum(own, got):
    half = own.shape[0] // 2
    return pl.pallas_call(
        line_kernel,
        out_shape=[
            jax.ShapeDtypeStruct((half, TILE), jnp.float32),
            jax.ShapeDtypeStruct((half, TILE), jnp.bfloat16),
        ],
        in_specs=[vm()] * 4,
        out_specs=[vm()] * 2,
        scratch_shapes=[pltpu.VMEM(own.shape, jnp.float32)],
        compiler_params=params(),
        name="line_sum",
    )(own, *got)


def halve_kernel(own, got, keep, send):
    size = keep.shape[0]
    total = own[...] + got[...].astype(jnp.float32)
    keep[...] = total[:size]
    send[...] = total[size:].astype(jnp.bfloat16)


def halve_sum(own, got):
    half = own.shape[0] // 2
    return pl.pallas_call(
        halve_kernel,
        out_shape=[
            jax.ShapeDtypeStruct((half, TILE), jnp.float32),
            jax.ShapeDtypeStruct((half, TILE), jnp.bfloat16),
        ],
        in_specs=[vm()] * 2,
        out_specs=[vm()] * 2,
        compiler_params=params(),
        name="halve_sum",
    )(own, got)


def last_kernel(factor, own, got, out):
    out[...] = (own[...] + got[...].astype(jnp.float32)) * factor


def last_sum(factor, own, got):
    return pl.pallas_call(
        functools.partial(last_kernel, factor),
        out_shape=jax.ShapeDtypeStruct(own.shape, jnp.float32),
        in_specs=[vm()] * 2,
        out_specs=vm(),
        compiler_params=params(),
        name="last_sum",
    )(own, got)


def swap(value):
    return lax.ppermute(value, "samp", [(s, s ^ 1) for s in range(16)])


def trade(value, p):
    return lax.ppermute(value, "samp", round_pairs(p))


def after(value, *first):
    return lax.optimization_barrier((value, *first))[0]


def shards(tiles, omega, tile_rows, tile_cols, tile_count):
    kmers = lax.axis_size("kmer")
    other, held, table, lists = forward_first(tile_rows, tile_cols, tile_count, tiles, omega)
    sends = pair_sum(forward_next(NEAR_EARLY, lists, held, table), swap(other))
    held_late = after(held, *sends)
    parts = [trade(s, p) for p, s in enumerate(sends)]
    other = forward_next(FAR_LATE, lists, held_late, table)
    sends = pair_sum(forward_next(NEAR_LATE, lists, held_late, table), swap(other))
    parts += [trade(s, p + 2) for p, s in enumerate(sends)]
    turned = turn(tile_count, after(held, *sends))
    part = part_sum("part_sum", *parts)
    part, turned = lax.optimization_barrier((part, turned))
    chunk = part_sum("chunk_sum", part, swap(part))
    near = [trade(chunk, p) for p in range(4)]
    far = [swap(piece) for piece in near]
    first = backward_early(lists, turned, near[:2], far[:2])
    keep, *shares = backward_late(lists, turned, first, near[2:], far[2:])
    sketch = sketch_rows(after(chunk, *shares))
    got = [lax.ppermute(s, ("kmer", "samp"), y_pairs(r)) for r, s in enumerate(shares)]
    keep, share = line_sum(keep, got)
    keep, share = halve_sum(keep, lax.ppermute(share, "kmer", [(i, i ^ 1) for i in range(16)]))
    got = lax.ppermute(share, "kmer", [(i, i // 4 * 4 + 3 - i % 4) for i in range(16)])
    factor = 1.0 / (KB_DEV * TILE * kmers) ** 0.5
    return sketch, last_sum(factor, keep, got)


def solution(mesh):
    placed = (
        P(("kmer", "samp"), None, None),
        P("samp", None),
        P(("kmer", "samp")),
        P(("kmer", "samp")),
        P(("kmer", "samp")),
    )
    return jax.shard_map(
        shards,
        mesh=mesh,
        in_specs=placed,
        out_specs=(P(("kmer", "samp"), None), P(("samp", "kmer"), None)),
        check_vma=False,
    )
```

```python
import functools

import jax
import jax.numpy as jnp
from jax import lax
from jax.experimental import pallas as pl
from jax.experimental.pallas import tpu as pltpu
from jax.sharding import PartitionSpec as P

TILE = 128
KB_DEV = 56
SB_DEV = 8
CHUNK_BLOCKS = KB_DEV // 8
CHUNK = CHUNK_BLOCKS * TILE
PART_BLOCKS = 2 * CHUNK_BLOCKS
PART = PART_BLOCKS * TILE
UNROLL = 12
LIST = 128
FETCH = 8
VMEM_LIMIT = 48 * 1024 * 1024
COST = pl.CostEstimate(flops=200 * 44 * TILE**3, bytes_accessed=200 * 44 * TILE**2, transcendentals=0)

ROUNDS = (
    ((1, 0), (3, 1)),
    ((2, 0), (2, 1)),
    ((3, 0), (1, 1)),
    ((0, 0), (0, 1)),
)
NEAR_EARLY, NEAR_LATE, FAR_EARLY, FAR_LATE = range(4)
LINE = ((2, 2), (1, 3), (3, 1))
HIGH = ((2, 2), (1, 3), (3, 1))


def vm():
    return pl.BlockSpec(memory_space=pltpu.VMEM)


def sm():
    return pl.BlockSpec(memory_space=pltpu.SMEM)


def params():
    return pltpu.CompilerParams(vmem_limit_bytes=VMEM_LIMIT)


def place():
    j = lax.axis_index("samp")
    return j // 8, (j // 2) % 4, j % 2


def kmer_place():
    i = lax.axis_index("kmer")
    return i // 4, i % 4


def round_pairs(p):
    out = []
    for s in range(16):
        z, x, c = s // 8, (s // 2) % 4, s % 2
        dx, dz = ROUNDS[p][c]
        out.append((s, (z ^ dz) * 8 + (x ^ dx) * 2 + c))
    return out


def y_pairs(r):
    out = []
    for i in range(16):
        for j in range(16):
            to = ((i // 4 + LINE[r][j % 2]) % 4) * 4 + i % 4
            out.append((i * 16 + j, to * 16 + j))
    return out


def block(i):
    return pl.ds(pl.multiple_of(i * TILE, TILE), TILE)


def chunk_at(q):
    return pl.ds(q * CHUNK, CHUNK)


def unpack(word):
    return lax.rem(word, 128), lax.rem(lax.div(word, 128), 64), lax.div(word, 8192)


def size_of(lists, which):
    return lists[which * LIST + LIST - 1]


def list_slots(rows, cols, count, lists, shift, owner):
    cap = rows.shape[0]
    z, x, c = place()
    for m in range(8):
        mx = m % 4
        e = jnp.bitwise_xor(x, mx)
        same_z = (z == m // 4).astype(jnp.int32)
        core = 1 - same_z
        odd = jnp.where(core == 0, e == 3, e == 1).astype(jnp.int32)
        p = jnp.where(e == 0, 3, jnp.where(e == 2, 1, 2 * odd))
        late = (p >= 2).astype(jnp.int32)
        shift[m] = (p - 2 * late - m) * CHUNK_BLOCKS
        owner[m] = jnp.where(core == c, 0, 2) + late

    def visit(s, sizes):
        row = rows[s]
        m = (row * 37) >> 8
        word = s + (row + shift[m]) * 128 + cols[s] * 8192
        which = jnp.where(s < count, owner[m], 4)
        for k, n in enumerate(sizes):
            lists[k * LIST + n] = word
        return tuple(n + (which == k).astype(jnp.int32) for k, n in enumerate(sizes))

    sizes = lax.fori_loop(0, cap, visit, (jnp.int32(0),) * 4, unroll=8)
    for k, n in enumerate(sizes):
        pad = lax.rem(lists[k * LIST], 128) + PART_BLOCKS * 128 + SB_DEV * 8192
        for u in range(UNROLL):
            lists[k * LIST + n + u] = pad
        lists[k * LIST + LIST - 1] = n


def forward_slots(lists, which, tiles, omega, acc, out):
    acc[...] = jnp.zeros_like(acc)

    def step(g, carry):
        prods, where = [], []
        for u in range(UNROLL):
            slot, row, col = unpack(lists[which * LIST + g * UNROLL + u])
            col = jnp.minimum(col, SB_DEV - 1)
            where.append(block(row))
            prods.append(
                jnp.dot(tiles[slot], omega[block(col), :], preferred_element_type=jnp.float32)
            )
        for at, prod in zip(where, prods):
            acc[at, :] = acc[at, :] + prod
        return carry

    lax.fori_loop(0, (size_of(lists, which) + UNROLL - 1) // UNROLL, step, 0)
    out[...] = acc[pl.ds(0, PART), :].astype(jnp.bfloat16)


def forward_first_kernel(
    rows, cols, count, tiles, omega, out, held, table, lists, acc, s_rows, s_cols, shift, owner, sems, tile_sems
):
    small = [
        pltpu.make_async_copy(rows, s_rows, sems.at[0]),
        pltpu.make_async_copy(cols, s_cols, sems.at[1]),
    ]
    for copy in small:
        copy.start()
    used = count[0]

    def fetch(g):
        at = pl.ds(g * FETCH, FETCH)
        return pltpu.make_async_copy(tiles.at[at], held.at[at], tile_sems.at[g])

    fetches = tiles.shape[0] // FETCH
    for g in range(fetches):
        pl.when(g * FETCH < used)(fetch(g).start)
    fetch_omega = pltpu.make_async_copy(omega, table, sems.at[2])
    fetch_omega.start()
    for copy in small:
        copy.wait()
    list_slots(s_rows, s_cols, used, lists, shift, owner)
    for g in range(fetches):
        pl.when(g * FETCH < used)(fetch(g).wait)
    fetch_omega.wait()
    forward_slots(lists, FAR_EARLY, held, table, acc, out)


def in_hbm(value):
    return pltpu.with_memory_space_constraint(value, pltpu.HBM)


def forward_first(rows, cols, count, tiles, omega):
    cap = tiles.shape[0]
    anywhere = pl.BlockSpec(memory_space=pltpu.HBM)
    return pl.pallas_call(
        forward_first_kernel,
        out_shape=[
            jax.ShapeDtypeStruct((PART, TILE), jnp.bfloat16),
            jax.ShapeDtypeStruct(tiles.shape, tiles.dtype),
            jax.ShapeDtypeStruct(omega.shape, omega.dtype),
            jax.ShapeDtypeStruct((4 * LIST,), jnp.int32),
        ],
        in_specs=[anywhere, anywhere, sm(), anywhere, anywhere],
        out_specs=[vm(), vm(), vm(), sm()],
        scratch_shapes=[
            pltpu.VMEM((PART + TILE, TILE), jnp.float32),
            pltpu.SMEM((cap,), jnp.int32),
            pltpu.SMEM((cap,), jnp.int32),
            pltpu.SMEM((8,), jnp.int32),
            pltpu.SMEM((8,), jnp.int32),
            pltpu.SemaphoreType.DMA((3,)),
            pltpu.SemaphoreType.DMA((cap // FETCH,)),
        ],
        compiler_params=params(),
        name="forward_first",
    )(in_hbm(rows), in_hbm(cols), count, in_hbm(tiles), in_hbm(omega))


def forward_next_kernel(which, lists, held, table, out, acc):
    forward_slots(lists, which, held, table, acc, out)


def forward_next(which, lists, held, table):
    return pl.pallas_call(
        functools.partial(forward_next_kernel, which),
        out_shape=jax.ShapeDtypeStruct((PART, TILE), jnp.bfloat16),
        in_specs=[sm(), vm(), vm()],
        out_specs=vm(),
        scratch_shapes=[pltpu.VMEM((PART + TILE, TILE), jnp.float32)],
        compiler_params=params(),
        cost_estimate=COST,
        name=f"forward_next{which}",
    )(lists, held, table)


def turn_kernel(count, tiles, out):
    def one(g, carry):
        for u in range(4):
            out[g * 4 + u] = tiles[g * 4 + u].T
        return carry

    lax.fori_loop(0, (count[0] + 3) // 4, one, 0)


def turn(count, tiles):
    return pl.pallas_call(
        turn_kernel,
        out_shape=jax.ShapeDtypeStruct(tiles.shape, tiles.dtype),
        in_specs=[sm(), vm()],
        out_specs=vm(),
        compiler_params=params(),
        name="turn_tiles",
    )(count, tiles)


def pair_kernel(a, b, *sends):
    for q, send in enumerate(sends):
        at = chunk_at(q)
        send[...] = (a[at, :].astype(jnp.float32) + b[at, :].astype(jnp.float32)).astype(jnp.bfloat16)


def pair_sum(a, b):
    shape = jax.ShapeDtypeStruct((CHUNK, TILE), jnp.bfloat16)
    return pl.pallas_call(
        pair_kernel,
        out_shape=[shape] * 2,
        in_specs=[vm(), vm()],
        out_specs=[vm()] * 2,
        compiler_params=params(),
        name="pair_sum",
    )(a, b)


def part_kernel(*refs):
    out = refs[-1]
    total = refs[0][...].astype(jnp.float32)
    for ref in refs[1:-1]:
        total = total + ref[...].astype(jnp.float32)
    out[...] = total.astype(jnp.bfloat16)


def part_sum(name, *parts):
    return pl.pallas_call(
        part_kernel,
        out_shape=jax.ShapeDtypeStruct((CHUNK, TILE), jnp.bfloat16),
        in_specs=[vm()] * len(parts),
        out_specs=vm(),
        compiler_params=params(),
        name=name,
    )(*parts)


def backward_slots(lists, which, turned, table, acc):
    def step(g, carry):
        prods, where = [], []
        for u in range(UNROLL):
            slot, row, col = unpack(lists[which * LIST + g * UNROLL + u])
            row = jnp.minimum(row, PART_BLOCKS - 1)
            where.append(block(col))
            prods.append(
                jnp.dot(turned[slot], table[block(row), :], preferred_element_type=jnp.float32)
            )
        for at, prod in zip(where, prods):
            acc[at, :] = acc[at, :] + prod
        return carry

    lax.fori_loop(0, (size_of(lists, which) + UNROLL - 1) // UNROLL, step, 0)


def backward_part(lists, kinds, turned, near, far, table, acc):
    for kind, pieces in zip(kinds, (near, far)):
        for q, piece in enumerate(pieces):
            table[chunk_at(q), :] = piece[...]
        backward_slots(lists, kind, turned, table, acc)


def sketch_kernel(chunk, out):
    _, _, c = place()
    size = out.shape[0]
    out[...] = chunk[pl.ds(pl.multiple_of(c * size, size), size), :]


def sketch_rows(chunk):
    return pl.pallas_call(
        sketch_kernel,
        out_shape=jax.ShapeDtypeStruct((CHUNK // 2, TILE), jnp.bfloat16),
        in_specs=[vm()],
        out_specs=vm(),
        compiler_params=params(),
        name="sketch_rows",
    )(chunk)


def backward_early_kernel(lists, turned, n0, n1, f0, f1, out, table):
    out[...] = jnp.zeros_like(out)
    backward_part(lists, (NEAR_EARLY, FAR_EARLY), turned, (n0, n1), (f0, f1), table, out)


def backward_early(lists, turned, near, far):
    return pl.pallas_call(
        backward_early_kernel,
        out_shape=jax.ShapeDtypeStruct(((SB_DEV + 1) * TILE, TILE), jnp.float32),
        in_specs=[sm()] + [vm()] * 5,
        out_specs=vm(),
        scratch_shapes=[pltpu.VMEM((PART, TILE), jnp.bfloat16)],
        compiler_params=params(),
        cost_estimate=COST,
        name="backward_early",
    )(lists, turned, *near, *far)


def line_offset(r):
    _, _, c = place()
    return jnp.where(c == 0, LINE[r][0], LINE[r][1])


def share_at(i, size):
    return pl.ds(pl.multiple_of(lax.rem(i + 4, 4) * size, size), size)


def backward_late_kernel(lists, turned, first, n2, n3, f2, f3, keep, s0, s1, s2, acc, table):
    acc[...] = first[...]
    backward_part(lists, (NEAR_LATE, FAR_LATE), turned, (n2, n3), (f2, f3), table, acc)
    y, _ = kmer_place()
    size = keep.shape[0]
    for r, send in enumerate((s0, s1, s2)):
        send[...] = acc[share_at(y + line_offset(r), size), :].astype(jnp.bfloat16)
    keep[...] = acc[share_at(y, size), :]


def backward_late(lists, turned, first, near, far):
    share = SB_DEV * TILE // 4
    send = jax.ShapeDtypeStruct((share, TILE), jnp.bfloat16)
    return pl.pallas_call(
        backward_late_kernel,
        out_shape=[jax.ShapeDtypeStruct((share, TILE), jnp.float32), send, send, send],
        in_specs=[sm()] + [vm()] * 6,
        out_specs=[vm()] * 4,
        scratch_shapes=[
            pltpu.VMEM(((SB_DEV + 1) * TILE, TILE), jnp.float32),
            pltpu.VMEM((PART, TILE), jnp.bfloat16),
        ],
        compiler_params=params(),
        name="backward_late",
    )(lists, turned, first, *near, *far)


def line_kernel(own, g0, g1, g2, keep, s0, s1, s2, acc):
    total = own[...]
    for got in (g0, g1, g2):
        total = total + got[...].astype(jnp.float32)
    acc[...] = total
    _, zh = kmer_place()
    _, _, c = place()
    size = keep.shape[0]
    for moves, send in zip(HIGH, (s0, s1, s2)):
        peer = jnp.bitwise_xor(zh, jnp.where(c == 0, moves[0], moves[1]))
        send[...] = acc[share_at(peer, size), :].astype(jnp.bfloat16)
    keep[...] = acc[share_at(zh, size), :]


def line_sum(own, got):
    share = own.shape[0] // 4
    send = jax.ShapeDtypeStruct((share, TILE), jnp.bfloat16)
    return pl.pallas_call(
        line_kernel,
        out_shape=[jax.ShapeDtypeStruct((share, TILE), jnp.float32), send, send, send],
        in_specs=[vm()] * 4,
        out_specs=[vm()] * 4,
        scratch_shapes=[pltpu.VMEM(own.shape, jnp.float32)],
        compiler_params=params(),
        name="line_sum",
    )(own, *got)


def last_kernel(factor, own, g0, g1, g2, out):
    total = own[...]
    for got in (g0, g1, g2):
        total = total + got[...].astype(jnp.float32)
    out[...] = total * factor


def last_sum(factor, own, got):
    return pl.pallas_call(
        functools.partial(last_kernel, factor),
        out_shape=jax.ShapeDtypeStruct(own.shape, jnp.float32),
        in_specs=[vm()] * 4,
        out_specs=vm(),
        compiler_params=params(),
        name="last_sum",
    )(own, *got)


def high_pairs(moves):
    return [
        (i * 16 + j, (i // 4 * 4 + (i % 4 ^ moves[j % 2])) * 16 + j)
        for i in range(16)
        for j in range(16)
    ]


def swap(value):
    return lax.ppermute(value, "samp", [(s, s ^ 1) for s in range(16)])


def trade(value, p):
    return lax.ppermute(value, "samp", round_pairs(p))


def after(value, *first):
    return lax.optimization_barrier((value, *first))[0]


def shards(tiles, omega, tile_rows, tile_cols, tile_count):
    kmers = lax.axis_size("kmer")
    other, held, table, lists = forward_first(tile_rows, tile_cols, tile_count, tiles, omega)
    sends = pair_sum(forward_next(NEAR_EARLY, lists, held, table), swap(other))
    held_late = after(held, *sends)
    parts = [trade(s, p) for p, s in enumerate(sends)]
    other = forward_next(FAR_LATE, lists, held_late, table)
    sends = pair_sum(forward_next(NEAR_LATE, lists, held_late, table), swap(other))
    parts += [trade(s, p + 2) for p, s in enumerate(sends)]
    turned = turn(tile_count, after(held, *sends))
    part = part_sum("part_sum", *parts)
    part, turned = lax.optimization_barrier((part, turned))
    chunk = part_sum("chunk_sum", part, swap(part))
    near = [trade(chunk, p) for p in range(4)]
    far = [swap(piece) for piece in near]
    first = backward_early(lists, turned, near[:2], far[:2])
    keep, *shares = backward_late(lists, turned, first, near[2:], far[2:])
    sketch = sketch_rows(after(chunk, *shares))
    got = [lax.ppermute(s, ("kmer", "samp"), y_pairs(r)) for r, s in enumerate(shares)]
    keep, *shares = line_sum(keep, got)
    got = [lax.ppermute(s, ("kmer", "samp"), high_pairs(m)) for s, m in zip(shares, HIGH)]
    factor = 1.0 / (KB_DEV * TILE * kmers) ** 0.5
    return sketch, last_sum(factor, keep, got)


def solution(mesh):
    placed = (
        P(("kmer", "samp"), None, None),
        P("samp", None),
        P(("kmer", "samp")),
        P(("kmer", "samp")),
        P(("kmer", "samp")),
    )
    return jax.shard_map(
        shards,
        mesh=mesh,
        in_specs=placed,
        out_specs=(P(("kmer", "samp"), None), P(("samp", "kmer"), None)),
        check_vma=False,
    )
```
